32 devices in a mesh: groups: 1, ctx: 16 (over z, y, x), tp: 2 (over core).
Axes of the slice: x: 2, y: 2, z: 4, core: 2. Of those that a mesh axis runs over, the one named last changes fastest.
Arguments:
- queries: bfloat16 [4, 32, 64, 128], P('groups', 'ctx', 'tp'), may hold values from -100 to 100
- cand_keys: bfloat16 [4, 32, 8, 128], P('groups', 'ctx', 'tp'), may hold values from -4 to 4
- candidate_values: bfloat16 [4, 32, 8, 128], P('groups', 'ctx', 'tp'), may hold values from -5 to 5
- cached_prompt_keys: bfloat16 [256, 128, 8, 128], P(('groups', 'ctx'), None, 'tp'), may hold values from -4 to 4
- cached_prompt_values: bfloat16 [256, 128, 8, 128], P(('groups', 'ctx'), None, 'tp'), may hold values from -5 to 5
- block_lists: int32 [4, 128], P('groups'), may hold values from 0 to 255, as said below
- out_weight: bfloat16 [8192, 8192], P('tp', 'ctx'), may hold values from -0.0625 to 0.0625
Outputs:
- verified: bfloat16 [4, 32, 8192], P('groups', 'tp', 'ctx')
The draws below stay inside these ranges and needn't reach their ends.
Inputs may be any that keep to these rules, and one draw needn't show every extreme that they name: `block_lists`: each row holds 128 distinct block numbers in increasing order; among blocks 16 * c to 16 * (c + 1) - 1 a row has at most 16 entries, exactly 16 for some c in every row; all rows together have at most 40 entries in one such range, exactly 40 in some.
All inputs are finite; a program needn't handle non-finite values.
Results may differ from the reference program's by a relative error of at most 0.022.
Values may be sent and summed in bfloat16 or wider, within the bound.
A program may use at most 128 MiB of HBM per device.

```python
import jax
import jax.numpy as jnp
from jax import lax

D = 8192
QUERY_HEADS = 64
KEY_VALUE_HEADS = 8
HEAD_WIDTH = 128
PROMPT_BLOCK = 128
READ_BLOCKS = 128
CANDIDATE_COUNT = 4
BLK_DEV = 16
PROMPT_BLOCKS = 256
CANDIDATE_LENGTH = 32


def paired_draw(key):
    base = jax.random.fold_in(key, 7)
    key_one, random_key_second = jax.random.split(base, 2)
    candidate_own_keys = jnp.clip(jax.random.normal(random_key_second, (CANDIDATE_COUNT, CANDIDATE_LENGTH, KEY_VALUE_HEADS, HEAD_WIDTH), jnp.float32), -4.0, 4.0)
    query_matrix = jnp.clip(jax.random.normal(key_one, (CANDIDATE_COUNT, CANDIDATE_LENGTH, QUERY_HEADS, HEAD_WIDTH), jnp.float32), -4.0, 4.0)
    return (query_matrix, candidate_own_keys)


def draw_queries(key, part):
    return paired_draw(key)[0].astype(jnp.bfloat16)


def draw_cand_keys(key, part):
    return paired_draw(key)[1].astype(jnp.bfloat16)


def draw_block_lists(key, part):
    ranges = PROMPT_BLOCKS // BLK_DEV
    most = min(BLK_DEV, 4 * READ_BLOCKS // ranges)
    second = most // 2
    base = jax.random.fold_in(key, 11)
    busiest = jax.random.permutation(jax.random.fold_in(base, 1), ranges)[:CANDIDATE_COUNT]

    def candidate(index):
        own_key = jax.random.fold_in(base, 100 + index)
        key_one, random_key_second = jax.random.split(own_key)
        device = jnp.arange(ranges)
        is_busy = device == busiest[index]
        forced = (device == busiest[0]) & (index > 0)
        remaining = READ_BLOCKS - most - jnp.where(index > 0, second, 0)
        scores = jax.random.permutation(key_one, ranges * second).reshape(ranges, second)
        eligible = jnp.logical_not(is_busy | forced)
        scores = jnp.where(eligible[:, None], scores, ranges * second + 1)
        ranking = jnp.argsort(jnp.argsort(scores.reshape(-1))).reshape(ranges, second)
        chosen = ranking < remaining
        counts = jnp.where(is_busy, most, jnp.where(forced, second, jnp.sum(chosen.astype(jnp.int32), axis=1)))
        orders = jax.vmap(lambda sub: jax.random.permutation(sub, BLK_DEV))(jax.random.split(random_key_second, ranges))[:, :most]
        blocks = device[:, None] * BLK_DEV + orders
        slot = jnp.arange(most)
        marked = jnp.where(slot[None, :] < counts[:, None], blocks, PROMPT_BLOCKS + 1)
        return jnp.sort(marked.reshape(-1))[:READ_BLOCKS].astype(jnp.int32)
    return jax.vmap(candidate)(jnp.arange(CANDIDATE_COUNT))


def block_levels(rng, dims, pieces, smallest, largest):
    gain, own = 1.0, jax.random.fold_in(rng, 6)
    for dim, blocks in pieces:
        heights = jnp.exp(jax.random.uniform(jax.random.fold_in(own, dim), (blocks,), jnp.float32, smallest / len(pieces), largest / len(pieces)))
        gain = gain * jnp.repeat(heights, dims[dim] // blocks).reshape([-1 if axis == dim else 1 for axis in range(len(dims))])
    return gain


def scatter_about(key, extent, spread, limit, pieces=(), kind=jnp.bfloat16):
    result = spread * jax.random.normal(key, extent, jnp.float32)
    if pieces:
        result = result * block_levels(key, extent, pieces, -0.22, 0.18)
    return jnp.clip(result, -limit, limit).astype(kind)


def setup_inputs(seed: int = 0, part: int = 0) -> dict:
    streams_of = jax.random.split(jax.random.key(seed), 8)
    own_keys = jax.random.split(jax.random.fold_in(streams_of[7], part), 8)
    queries = draw_queries(jax.random.fold_in(jax.random.fold_in(streams_of[7], part), 71), part)
    cand_keys = draw_cand_keys(jax.random.fold_in(jax.random.fold_in(streams_of[7], part), 71), part)
    candidate_values = scatter_about(own_keys[2], (CANDIDATE_COUNT, CANDIDATE_LENGTH, KEY_VALUE_HEADS, HEAD_WIDTH), 1.0, 5.0, ((1, 16), (2, 2)))
    cached_prompt_keys = scatter_about(own_keys[3], (PROMPT_BLOCKS, PROMPT_BLOCK, KEY_VALUE_HEADS, HEAD_WIDTH), 1.0, 4.0, ((0, 16), (2, 2)))
    cached_prompt_values = scatter_about(own_keys[4], (PROMPT_BLOCKS, PROMPT_BLOCK, KEY_VALUE_HEADS, HEAD_WIDTH), 1.0, 5.0, ((0, 16), (2, 2)))
    block_lists = draw_block_lists(jax.random.fold_in(jax.random.fold_in(streams_of[7], part), 71), part)
    out_weight = scatter_about(streams_of[6], (QUERY_HEADS * HEAD_WIDTH, D), (QUERY_HEADS * HEAD_WIDTH) ** -0.5, 0.0625, ((0, 2), (1, 16)))
    return dict(queries=queries, cand_keys=cand_keys, candidate_values=candidate_values, cached_prompt_keys=cached_prompt_keys, cached_prompt_values=cached_prompt_values, block_lists=block_lists, out_weight=out_weight)


def reference(queries, cand_keys, candidate_values, cached_prompt_keys, cached_prompt_values, block_lists, out_weight):
    query_group_width = QUERY_HEADS // KEY_VALUE_HEADS
    factor = HEAD_WIDTH ** -0.5
    position = jnp.arange(CANDIDATE_LENGTH)
    causal = position[None, :] <= position[:, None]
    visible = jnp.concatenate([jnp.ones((CANDIDATE_LENGTH, READ_BLOCKS * PROMPT_BLOCK), dtype=bool), causal], axis=1)

    def candidate(inputs):
        query_matrix, candidate_own_keys, own_values, listed_blocks = inputs
        gathered_keys = jnp.take(cached_prompt_keys, listed_blocks, axis=0).reshape(READ_BLOCKS * PROMPT_BLOCK, KEY_VALUE_HEADS, HEAD_WIDTH)
        gathered_values = jnp.take(cached_prompt_values, listed_blocks, axis=0).reshape(READ_BLOCKS * PROMPT_BLOCK, KEY_VALUE_HEADS, HEAD_WIDTH)
        all_keys = jnp.concatenate([gathered_keys, candidate_own_keys], axis=0)
        all_values = jnp.concatenate([gathered_values, own_values], axis=0)
        grouped_queries = query_matrix.reshape(CANDIDATE_LENGTH, KEY_VALUE_HEADS, query_group_width, HEAD_WIDTH)

        def kv_head(parts):
            head_queries, head_keys, head_values = parts
            scores = jnp.einsum('ngd,md->gnm', head_queries.astype(jnp.float32), head_keys.astype(jnp.float32)) * factor
            scores = jnp.where(visible[None], scores, -1e30)
            maxima = jnp.max(scores, axis=-1, keepdims=True)
            expon = jnp.where(visible[None], jnp.exp(scores - maxima), 0.0)
            denominator = jnp.sum(expon, axis=-1)
            rounded = lax.optimization_barrier(expon.astype(jnp.bfloat16)).astype(jnp.float32)
            numerator = jnp.einsum('gnm,md->ngd', rounded, head_values.astype(jnp.float32))
            return numerator / jnp.transpose(denominator)[:, :, None]

        heads_out = lax.map(kv_head, (jnp.transpose(grouped_queries, (1, 0, 2, 3)), jnp.transpose(all_keys, (1, 0, 2)), jnp.transpose(all_values, (1, 0, 2))))
        return jnp.transpose(heads_out, (1, 0, 2, 3)).reshape(CANDIDATE_LENGTH, QUERY_HEADS * HEAD_WIDTH).astype(jnp.bfloat16)

    attention = lax.map(candidate, (queries, cand_keys, candidate_values, block_lists))
    product = jnp.dot(attention.reshape(CANDIDATE_COUNT * CANDIDATE_LENGTH, QUERY_HEADS * HEAD_WIDTH), out_weight, preferred_element_type=jnp.float32)
    return product.astype(jnp.bfloat16).reshape(CANDIDATE_COUNT, CANDIDATE_LENGTH, D)
```

```python
import functools
import math

import jax
import jax.numpy as jnp
from jax import lax
from jax.experimental import pallas as pl
from jax.experimental.pallas import tpu as pltpu
from jax.sharding import PartitionSpec as P

NEGATIVE = -1e30
MESH = pl.DeviceIdType.MESH
F32, BF16 = jnp.float32, jnp.bfloat16


class Place:
    def __init__(self, ranges):
        self.me = lax.axis_index("ctx")
        self.depth = ranges // 4
        self.x, self.y, self.z = self.me % 2, (self.me // 2) % 2, self.me // 4
        self.beside_x = self.at(self.z, self.y, 1 - self.x)
        self.beside_y = self.at(self.z, 1 - self.y, self.x)

    def at(self, z, y, x):
        return z * 4 + y * 2 + x

    def shifted(self, d):
        return (self.z + d + self.depth) % self.depth

    def line(self, d):
        return self.at(self.shifted(d), self.y, self.x)


def greet(place, with_tp):
    barrier = pltpu.get_barrier_semaphore()
    others = [place.line(d) for d in range(1, place.depth)]
    for other in others + [place.beside_x, place.beside_y]:
        pl.semaphore_signal(barrier, inc=1, device_id={"ctx": other}, device_id_type=MESH)
    if with_tp:
        pl.semaphore_signal(
            barrier, inc=1, device_id={"tp": 1 - lax.axis_index("tp")}, device_id_type=MESH
        )
    pl.semaphore_wait(barrier, place.depth + 1 + int(with_tp))


def gather_pieces(place, buf, send, recv):
    def copy(kind, d, owner, target):
        return pltpu.make_async_remote_copy(
            src_ref=buf.at[owner],
            dst_ref=buf.at[owner],
            send_sem=send.at[kind, d],
            recv_sem=recv.at[kind, d],
            device_id={"ctx": target},
            device_id_type=MESH,
        )

    sent = []

    def go(*what):
        one = copy(*what)
        one.start()
        sent.append(one)

    depth = place.depth
    z_of = [place.shifted(-d) for d in range(depth)]

    def spread(d):
        owner = place.at(z_of[d], place.y, place.x)
        if d:
            copy(0, d, owner, place.me).wait_recv()
        go(1, d, owner, place.beside_x)
        go(2, d, owner, place.beside_y)

    def relay(d):
        from_x = place.at(z_of[d], place.y, 1 - place.x)
        from_y = place.at(z_of[d], 1 - place.y, place.x)
        copy(1, d, from_x, place.me).wait_recv()
        if d % 2 == 0:
            go(3, d, from_x, place.beside_y)
        copy(2, d, from_y, place.me).wait_recv()
        if d % 2 == 1:
            go(3, d, from_y, place.beside_x)

    for d in range(1, depth):
        go(0, d, place.me, place.line(d))
    spread(0)
    for d in range(1, depth):
        spread(d)
        relay(d - 1)
    relay(depth - 1)
    for d in range(depth):
        copy(3, d, place.at(z_of[d], 1 - place.y, 1 - place.x), place.me).wait_recv()
    for one in sent:
        one.wait_send()


def query_kernel(ranges, q_ref, out_ref, send, recv):
    place = Place(ranges)
    out_ref[place.me] = q_ref[...]
    greet(place, False)
    gather_pieces(place, out_ref, send, recv)


def attend_kernel(
    sizes,
    lists_smem,
    lists_ref,
    q_ref,
    own_k_ref,
    own_v_ref,
    k_ref,
    v_ref,
    out_ref,
    wide,
    k_heads,
    v_heads,
    scores,
    sums,
    acc,
    top,
):
    cands, toks, kv, group, blocks, block_tokens, head, tile_owners = sizes
    chunk = pl.program_id(0)
    me = lax.axis_index("ctx")
    scale = head ** (-0.5) * math.log2(math.e)
    rows = tile_owners * toks * group
    lowest = me * blocks

    @pl.when(chunk == 0)
    def _():
        def spread(b, carry):
            for src, dst in ((k_ref, k_heads), (v_ref, v_heads)):
                wide[...] = src[b].astype(F32)
                for h in range(kv):
                    dst[h, b] = wide[pl.ds(h, block_tokens, stride=kv), :].astype(BF16)
            return carry

        lax.fori_loop(0, blocks, spread, 0)

    row = lax.broadcasted_iota(jnp.int32, (rows, block_tokens), 0)
    lane = lax.broadcasted_iota(jnp.int32, (rows, block_tokens), 1)
    query_pos = chunk * tile_owners * toks + row // group
    own_seen = (lane < toks) & (me * toks + lane <= query_pos)
    stats = jnp.zeros((rows, 128), F32)
    lanes = lax.broadcasted_iota(jnp.int32, (rows, 128), 1)
    nt = (((1,), (1,)), ((), ()))
    for j in range(cands):
        line = lists_ref[j : j + 1, :]
        below = jnp.sum((line < lowest).astype(jnp.int32))
        count = jnp.sum((line < lowest + blocks).astype(jnp.int32)) - below
        last = lists_smem.shape[1] - 1

        def pair_of(i):
            first = lists_smem[j, jnp.minimum(below + 2 * i, last)] - lowest
            second = lists_smem[j, jnp.minimum(below + 2 * i + 1, last)] - lowest
            inside = 2 * i + 1 < count
            return first, jnp.where(inside, second, first), inside

        queries = []
        for h in range(kv):
            q = q_ref[:, j, :, h * group : (h + 1) * group, :].astype(F32)
            queries.append(q.reshape(rows, head).astype(BF16))
            own = lax.dot_general(
                queries[h], own_k_ref[h, j], nt, preferred_element_type=F32
            )
            own = jnp.where(own_seen, own, NEGATIVE)
            sums[h] = own
            top[h] = own

        def first_pass(i, carry):
            a, b, inside = pair_of(i)
            for h in range(kv):
                keys = jnp.concatenate([k_heads[h, a], k_heads[h, b]], axis=0)
                s = lax.dot_general(queries[h], keys, nt, preferred_element_type=F32)
                left = s[:, :block_tokens]
                right = jnp.where(inside, s[:, block_tokens:], NEGATIVE)
                scores[h, i, :, :block_tokens] = left
                scores[h, i, :, block_tokens:] = right
                top[h] = jnp.maximum(top[h], jnp.maximum(left, right))
            return carry

        pairs = (count + 1) // 2
        lax.fori_loop(0, pairs, first_pass, 0)
        for h in range(kv):
            peak = jnp.max(top[h], axis=1, keepdims=True).astype(BF16).astype(F32)
            p = jnp.where(own_seen, jnp.exp2((sums[h] - peak) * scale), 0.0)
            sums[h] = p
            acc[h] = jnp.dot(p.astype(BF16), own_v_ref[h, j], preferred_element_type=F32)
            top[h] = jnp.broadcast_to(peak, (rows, block_tokens))

        def second_pass(i, carry):
            a, b, _ = pair_of(i)
            for h in range(kv):
                values = jnp.concatenate([v_heads[h, a], v_heads[h, b]], axis=0)
                peak = top[h]
                left = jnp.exp2((scores[h, i, :, :block_tokens] - peak) * scale)
                right = jnp.exp2((scores[h, i, :, block_tokens:] - peak) * scale)
                sums[h] += left + right
                p = jnp.concatenate([left.astype(BF16), right.astype(BF16)], axis=1)
                acc[h] += jnp.dot(p, values, preferred_element_type=F32)
            return carry

        lax.fori_loop(0, pairs, second_pass, 0)
        for h in range(kv):
            combo = h * cands + j
            total = jnp.sum(sums[h], axis=1, keepdims=True)
            stats = jnp.where(lanes == combo, top[h], stats)
            stats = jnp.where(lanes == 64 + combo, total, stats)
            per = toks * group
            out_ref[:, combo * per : (combo + 1) * per, :] = (
                acc[h].reshape(tile_owners, per, head).astype(BF16)
            )
    per = toks * group
    full = kv * cands * per
    out_ref[:, full : full + per, :] = stats.reshape(tile_owners, per, 128).astype(BF16)


def merge(pieces, combos, per, scale):
    full = combos * per
    stats = [load(full, per).astype(F32) for load in pieces]
    peak = functools.reduce(jnp.maximum, stats)
    low = lax.broadcasted_iota(jnp.int32, (per, 128), 1) < 64
    scales = [jnp.exp2((jnp.where(low, s - peak, 0.0)) * scale) for s in stats]
    total = sum(pltpu.roll(w, 64, 1) * s for w, s in zip(scales, stats))
    sums = []
    for c in range(combos):
        sums.append(
            sum(
                load(c * per, per).astype(F32) * w[:, c : c + 1]
                for load, w in zip(pieces, scales)
            )
        )
    return sums, jnp.where(low, peak, total), total


def finish_kernel(
    ranges,
    sizes,
    parts_ref,
    weight_ref,
    out_ref,
    from_diag,
    from_x,
    from_y,
    from_line,
    to_diag,
    to_line,
    gathered,
    ordered,
    weight,
    total,
    away,
    arrived,
    weight_sem,
    red_send,
    red_recv,
    send,
    recv,
    tp_sems,
):
    cands, toks, kv, group, head = sizes
    place = Place(ranges)
    depth = place.depth
    per = toks * group
    combos = kv * cands
    scale = head ** (-0.5) * math.log2(math.e)
    fetch = pltpu.make_async_copy(weight_ref, weight, weight_sem)
    fetch.start()
    greet(place, True)

    sent = []

    def copy(kind, d, src, dst, target):
        return pltpu.make_async_remote_copy(
            src_ref=src,
            dst_ref=dst,
            send_sem=red_send.at[kind, d],
            recv_sem=red_recv.at[kind, d],
            device_id={"ctx": target},
            device_id_type=MESH,
        )

    def go(*what):
        one = copy(*what)
        one.start()
        sent.append(one)

    def arrive(kind, d, dst):
        copy(kind, d, dst, dst, place.me).wait_recv()

    def owner(d, flip_y, flip_x):
        y = 1 - place.y if flip_y else place.y
        x = 1 - place.x if flip_x else place.x
        return place.at(place.shifted(d), y, x)

    def loader(ref, *index):
        return lambda start, size: ref[(*index, pl.ds(start, size), slice(None))]

    def put(dst, d, sums, stats):
        for c in range(combos):
            dst[d, c * per : (c + 1) * per, :] = sums[c].astype(BF16)
        dst[d, combos * per : (combos + 1) * per, :] = stats.astype(BF16)

    order = list(range(1, depth)) + [0]
    for d in order:
        far = parts_ref.at[owner(d, 1, 1)]
        if d % 2 == 0:
            go(0, d, far, from_diag.at[d], place.beside_x)
        else:
            go(0, d, far, from_diag.at[d], place.beside_y)
    for d in order:
        if d % 2 == 0:
            go(1, d, parts_ref.at[owner(d, 0, 1)], from_x.at[d], place.beside_x)
        else:
            go(2, d, parts_ref.at[owner(d, 1, 0)], from_y.at[d], place.beside_y)
    for d in order:
        arrive(0, d, from_diag.at[d])
        mine = owner(d, 1, 0) if d % 2 == 0 else owner(d, 0, 1)
        sums, stats, _ = merge(
            (loader(parts_ref, mine), loader(from_diag, d)), combos, per, scale
        )
        put(to_diag, d, sums, stats)
        if d % 2 == 0:
            go(2, d, to_diag.at[d], from_y.at[d], place.beside_y)
        else:
            go(1, d, to_diag.at[d], from_x.at[d], place.beside_x)
    for d in order:
        arrive(1, d, from_x.at[d])
        arrive(2, d, from_y.at[d])
        sums, stats, _ = merge(
            (loader(parts_ref, owner(d, 0, 0)), loader(from_x, d), loader(from_y, d)),
            combos,
            per,
            scale,
        )
        put(to_line, d, sums, stats)
        if d:
            go(3, d, to_line.at[d], from_line.at[d], place.line(d))
    for d in range(1, depth):
        arrive(3, d, from_line.at[d])
    sums, _, denominator = merge(
        [loader(to_line, 0)] + [loader(from_line, d) for d in range(1, depth)],
        combos,
        per,
        scale,
    )
    denominator = pltpu.roll(denominator, 64, 1)
    for c in range(combos):
        ordered[c * per : (c + 1) * per, :] = sums[c] / denominator[:, c : c + 1]
    tokens = cands * toks
    for h in range(kv):
        block = [
            ordered[pl.ds(h * tokens * group + g, tokens, stride=group), :] for g in range(group)
        ]
        gathered[place.me, h * tokens * group : (h + 1) * tokens * group, :] = jnp.concatenate(
            block, axis=0
        ).astype(BF16)
    gather_pieces(place, gathered, send, recv)
    fetch.wait()
    total[...] = jnp.zeros_like(total)

    def project(i, carry):
        start = pl.multiple_of(i * 2 * tokens, 2 * tokens)
        both = gathered[:, pl.ds(start, 2 * tokens), :].astype(F32)
        left = both[:, :tokens, :].reshape(ranges * tokens, head).astype(BF16)
        right = both[:, tokens:, :].reshape(ranges * tokens, head).astype(BF16)
        rows = pl.multiple_of(i * 2 * head, 2 * head)
        total[...] += jnp.dot(
            jnp.concatenate([left, right], axis=1),
            weight[pl.ds(rows, 2 * head), :],
            preferred_element_type=F32,
        )
        return carry

    lax.fori_loop(0, kv * group // 2, project, 0)
    half = ranges * tokens // 2
    tp = lax.axis_index("tp")
    away[...] = total[pl.ds(pl.multiple_of((1 - tp) * half, half), half), :].astype(BF16)
    swap = pltpu.make_async_remote_copy(
        src_ref=away,
        dst_ref=arrived,
        send_sem=tp_sems.at[0],
        recv_sem=tp_sems.at[1],
        device_id={"tp": 1 - tp},
        device_id_type=MESH,
    )
    swap.start()
    for one in sent:
        one.wait_send()
    swap.wait()
    mine = total[pl.ds(pl.multiple_of(tp * half, half), half), :]
    out_ref[...] = (mine + arrived[...].astype(F32)).astype(BF16)


def on_device(
    queries,
    cand_keys,
    candidate_values,
    cached_prompt_keys,
    cached_prompt_values,
    block_lists,
    out_weight,
):
    cands, toks, heads, head = queries.shape
    kv = cand_keys.shape[2]
    group = heads // kv
    blocks, block_tokens = cached_prompt_keys.shape[:2]
    ranges = lax.axis_size("ctx")
    depth = ranges // 4
    piece = cands * toks * heads
    per = toks * group
    vmem = pl.BlockSpec(memory_space=pltpu.VMEM)
    limit = 60 * 1024 * 1024

    everyone = pl.pallas_call(
        functools.partial(query_kernel, ranges),
        out_shape=jax.ShapeDtypeStruct((ranges, piece, head), BF16),
        in_specs=[vmem],
        out_specs=vmem,
        scratch_shapes=[
            pltpu.SemaphoreType.DMA((4, depth)),
            pltpu.SemaphoreType.DMA((4, depth)),
        ],
        compiler_params=pltpu.CompilerParams(collective_id=0, has_side_effects=True),
        name="query_gather",
    )(queries.reshape(piece, head))

    tile_owners = min(ranges, 256 // per)
    rows = tile_owners * per
    own = [
        jnp.pad(
            jnp.transpose(a, (2, 0, 1, 3)), ((0, 0), (0, 0), (0, block_tokens - toks), (0, 0))
        )
        for a in (cand_keys, candidate_values)
    ]
    whole = lambda shape: pl.BlockSpec(
        shape, lambda i, *_: (0,) * len(shape), pipeline_mode=pl.Buffered(1)
    )
    own_spec = whole((kv, cands, block_tokens, head))
    cache_spec = whole((blocks, block_tokens * kv, head))
    sizes = (cands, toks, kv, group, blocks, block_tokens, head, tile_owners)
    parts = pl.pallas_call(
        functools.partial(attend_kernel, sizes),
        out_shape=jax.ShapeDtypeStruct((ranges, piece + per, head), BF16),
        grid_spec=pltpu.PrefetchScalarGridSpec(
            num_scalar_prefetch=1,
            grid=(ranges // tile_owners,),
            in_specs=[
                whole(block_lists.shape),
                pl.BlockSpec(
                    (tile_owners, cands, toks, heads, head), lambda i, *_: (i, 0, 0, 0, 0)
                ),
                own_spec,
                own_spec,
                cache_spec,
                cache_spec,
            ],
            out_specs=pl.BlockSpec((tile_owners, piece + per, head), lambda i, *_: (i, 0, 0)),
            scratch_shapes=[
                pltpu.VMEM((block_tokens * kv, head), F32),
                pltpu.VMEM((kv, blocks, block_tokens, head), BF16),
                pltpu.VMEM((kv, blocks, block_tokens, head), BF16),
                pltpu.VMEM((kv, (blocks + 1) // 2, rows, 2 * block_tokens), F32),
                pltpu.VMEM((kv, rows, block_tokens), F32),
                pltpu.VMEM((kv, rows, head), F32),
                pltpu.VMEM((kv, rows, block_tokens), F32),
            ],
        ),
        compiler_params=pltpu.CompilerParams(vmem_limit_bytes=limit),
        name="attend",
    )(
        block_lists,
        block_lists,
        everyone.reshape(ranges, cands, toks, heads, head),
        *own,
        cached_prompt_keys.reshape(blocks, block_tokens * kv, head),
        cached_prompt_values.reshape(blocks, block_tokens * kv, head),
    )

    columns = out_weight.shape[1]
    tokens = cands * toks
    half = ranges * tokens // 2
    block = pltpu.VMEM((depth, piece + per, head), BF16)
    result = pl.pallas_call(
        functools.partial(finish_kernel, ranges, (cands, toks, kv, group, head)),
        out_shape=jax.ShapeDtypeStruct((half, columns), BF16),
        in_specs=[vmem, pl.BlockSpec(memory_space=pl.ANY)],
        out_specs=vmem,
        scratch_shapes=[block] * 6
        + [
            pltpu.VMEM((ranges, piece, head), BF16),
            pltpu.VMEM((piece, head), F32),
            pltpu.VMEM(out_weight.shape, BF16),
            pltpu.VMEM((2 * half, columns), F32),
            pltpu.VMEM((half, columns), BF16),
            pltpu.VMEM((half, columns), BF16),
            pltpu.SemaphoreType.DMA,
            pltpu.SemaphoreType.DMA((4, depth)),
            pltpu.SemaphoreType.DMA((4, depth)),
            pltpu.SemaphoreType.DMA((4, depth)),
            pltpu.SemaphoreType.DMA((4, depth)),
            pltpu.SemaphoreType.DMA((2,)),
        ],
        compiler_params=pltpu.CompilerParams(
            collective_id=1, has_side_effects=True, vmem_limit_bytes=limit
        ),
        name="reduce_project",
    )(parts, out_weight)
    result = result.reshape(ranges // 2, cands, toks, columns)
    return jnp.transpose(result, (1, 0, 2, 3)).reshape(cands, ranges * toks // 2, columns)


def solution(mesh):
    placed = (
        P("groups", "ctx", "tp", None),
        P("groups", "ctx", "tp", None),
        P("groups", "ctx", "tp", None),
        P(("groups", "ctx"), None, "tp", None),
        P(("groups", "ctx"), None, "tp", None),
        P("groups", None),
        P("tp", "ctx"),
    )
    return jax.shard_map(
        on_device, mesh=mesh, in_specs=placed, out_specs=P("groups", "tp", "ctx"), check_vma=False
    )
```

```python
import functools
import math

import jax
import jax.numpy as jnp
from jax import lax
from jax.experimental import pallas as pl
from jax.experimental.pallas import tpu as pltpu
from jax.sharding import PartitionSpec as P

NEGATIVE = -1e30
MESH = pl.DeviceIdType.MESH
F32, BF16 = jnp.float32, jnp.bfloat16


class Place:
    def __init__(self, ranges):
        self.me = lax.axis_index("ctx")
        self.depth = ranges // 4
        self.x, self.y, self.z = self.me % 2, (self.me // 2) % 2, self.me // 4
        self.beside_x = self.at(self.z, self.y, 1 - self.x)
        self.beside_y = self.at(self.z, 1 - self.y, self.x)

    def at(self, z, y, x):
        return z * 4 + y * 2 + x

    def shifted(self, d):
        return (self.z + d + self.depth) % self.depth

    def line(self, d):
        return self.at(self.shifted(d), self.y, self.x)


def greet(place, with_tp):
    barrier = pltpu.get_barrier_semaphore()
    others = [place.line(d) for d in range(1, place.depth)]
    for other in others + [place.beside_x, place.beside_y]:
        pl.semaphore_signal(barrier, inc=1, device_id={"ctx": other}, device_id_type=MESH)
    if with_tp:
        pl.semaphore_signal(
            barrier, inc=1, device_id={"tp": 1 - lax.axis_index("tp")}, device_id_type=MESH
        )
    pl.semaphore_wait(barrier, place.depth + 1 + int(with_tp))


def near_first(depth):
    order = []
    for step in range(1, depth // 2 + 1):
        order += [step] + ([depth - step] if depth - step != step else [])
    return order


def gather_pieces(place, buf, send, recv, work=lambda step: None):
    def copy(kind, d, half, owner, target):
        return pltpu.make_async_remote_copy(
            src_ref=buf.at[owner, half],
            dst_ref=buf.at[owner, half],
            send_sem=send.at[kind, d, half],
            recv_sem=recv.at[kind, d, half],
            device_id={"ctx": target},
            device_id_type=MESH,
        )

    sent = []

    def go(*what):
        one = copy(*what)
        one.start()
        sent.append(one)

    depth = place.depth
    z_of = [place.shifted(-d) for d in range(depth)]

    def spread(d, half):
        owner = place.at(z_of[d], place.y, place.x)
        if d:
            copy(0, d, half, owner, place.me).wait_recv()
        go(1, d, half, owner, place.beside_x)
        go(2, d, half, owner, place.beside_y)

    def relay(d, half):
        from_x = place.at(z_of[d], place.y, 1 - place.x)
        from_y = place.at(z_of[d], 1 - place.y, place.x)
        if half == 0:
            copy(1, d, half, from_x, place.me).wait_recv()
            go(3, d, half, from_x, place.beside_y)
        else:
            copy(2, d, half, from_y, place.me).wait_recv()
            go(3, d, half, from_y, place.beside_x)

    def settle(d, half):
        from_x = place.at(z_of[d], place.y, 1 - place.x)
        from_y = place.at(z_of[d], 1 - place.y, place.x)
        if half == 0:
            copy(2, d, half, from_y, place.me).wait_recv()
        else:
            copy(1, d, half, from_x, place.me).wait_recv()
        across = place.at(z_of[d], 1 - place.y, 1 - place.x)
        copy(3, d, half, across, place.me).wait_recv()

    order = near_first(depth)
    for half in range(2):
        spread(0, half)
    for d in order:
        for half in range(2):
            go(0, d, half, place.me, place.line(d))
    work(0)
    steps = [(d, half) for d in [0] + order for half in range(2)]
    for i, step in enumerate(steps):
        if i + 2 < len(steps):
            spread(*steps[i + 2])
        relay(*step)
        work(i + 1)
    for step in steps:
        settle(*step)
    for one in sent:
        one.wait_send()


def query_kernel(
    ranges,
    kv,
    q_ref,
    k_ref,
    v_ref,
    out_ref,
    k_out,
    v_out,
    raw,
    wide,
    heads,
    send,
    recv,
    in_sems,
    out_sems,
):
    place = Place(ranges)
    sources, results = (k_ref, v_ref), (k_out, v_out)
    fetches = [pltpu.make_async_copy(sources[n], raw.at[n], in_sems.at[n]) for n in range(2)]
    for fetch in fetches:
        fetch.start()
    out_ref[place.me] = q_ref[...]
    greet(place, False)
    blocks, block_tokens = raw.shape[1], raw.shape[2] // kv
    parts = 4
    per = blocks // parts
    stores = []

    def work(step):
        if step >= 2 * parts:
            return
        n, part = step // parts, step % parts
        if part == 0:
            fetches[n].wait()

        def one(b, carry):
            wide[...] = raw[n, b].astype(F32)
            for h in range(kv):
                heads[n, h, b] = wide[pl.ds(h, block_tokens, stride=kv), :].astype(BF16)
            return carry

        lax.fori_loop(part * per, (part + 1) * per, one, 0)
        some = pl.ds(part * per, per)
        store = pltpu.make_async_copy(
            heads.at[n, :, some], results[n].at[:, some], out_sems.at[n, part]
        )
        store.start()
        stores.append(store)

    gather_pieces(place, out_ref, send, recv, work)
    for store in stores:
        store.wait()


def attend_kernel(
    sizes,
    lists_smem,
    lists_ref,
    q_ref,
    own_k_ref,
    own_v_ref,
    k_ref,
    v_ref,
    out_ref,
    k_heads,
    v_heads,
    scores,
    sums,
    acc,
    top,
    sems,
):
    cands, toks, kv, group, blocks, block_tokens, head, tile_owners = sizes
    chunk = pl.program_id(0)
    me = lax.axis_index("ctx")
    scale = head ** (-0.5) * math.log2(math.e)
    rows = tile_owners * toks * group
    lowest = me * blocks

    fetch_k = pltpu.make_async_copy(k_ref, k_heads, sems.at[0])
    fetch_v = pltpu.make_async_copy(v_ref, v_heads, sems.at[1])

    @pl.when(chunk == 0)
    def _():
        fetch_k.start()
        fetch_v.start()

    key_row = lax.broadcasted_iota(jnp.int32, (block_tokens, head), 0)

    def own_block(ref, h, j):
        rows_here = ref[j].astype(F32)
        block = jnp.zeros((block_tokens, head), F32)
        for t in range(toks):
            block = jnp.where(key_row == t, rows_here[t, h : h + 1, :], block)
        return block.astype(BF16)

    row = lax.broadcasted_iota(jnp.int32, (rows, block_tokens), 0)
    lane = lax.broadcasted_iota(jnp.int32, (rows, block_tokens), 1)
    query_pos = chunk * tile_owners * toks + row // group
    own_seen = (lane < toks) & (me * toks + lane <= query_pos)
    stats = [jnp.zeros((rows, 128), F32)] * 2
    per = toks * group
    lanes = lax.broadcasted_iota(jnp.int32, (rows, 128), 1)
    nt = (((1,), (1,)), ((), ()))
    for j in range(cands):
        line = lists_ref[j : j + 1, :]
        below = jnp.sum((line < lowest).astype(jnp.int32))
        count = jnp.sum((line < lowest + blocks).astype(jnp.int32)) - below
        last = lists_smem.shape[1] - 1

        def pair_of(i):
            first = lists_smem[j, jnp.minimum(below + 2 * i, last)] - lowest
            second = lists_smem[j, jnp.minimum(below + 2 * i + 1, last)] - lowest
            inside = 2 * i + 1 < count
            return first, jnp.where(inside, second, first), inside

        queries = []
        for h in range(kv):
            q = q_ref[:, j, :, h * group : (h + 1) * group, :].astype(F32)
            queries.append(q.reshape(rows, head).astype(BF16))
            own = lax.dot_general(
                queries[h], own_block(own_k_ref, h, j), nt, preferred_element_type=F32
            )
            own = jnp.where(own_seen, own, NEGATIVE)
            sums[h] = own
            top[h] = own

        if j == 0:
            pl.when(chunk == 0)(fetch_k.wait)

        def first_pass(i, carry):
            a, b, inside = pair_of(i)
            for h in range(kv):
                keys = jnp.concatenate([k_heads[h, a], k_heads[h, b]], axis=0)
                s = lax.dot_general(queries[h], keys, nt, preferred_element_type=F32)
                left = s[:, :block_tokens]
                right = jnp.where(inside, s[:, block_tokens:], NEGATIVE)
                scores[h, i, :, :block_tokens] = left
                scores[h, i, :, block_tokens:] = right
                top[h] = jnp.maximum(top[h], jnp.maximum(left, right))
            return carry

        pairs = (count + 1) // 2
        lax.fori_loop(0, pairs, first_pass, 0)
        for h in range(kv):
            peak = jnp.max(top[h], axis=1, keepdims=True).astype(BF16).astype(F32)
            p = jnp.where(own_seen, jnp.exp2((sums[h] - peak) * scale), 0.0)
            sums[h] = p
            acc[h] = jnp.dot(
                p.astype(BF16), own_block(own_v_ref, h, j), preferred_element_type=F32
            )
            top[h] = jnp.broadcast_to(peak, (rows, block_tokens))

        def second_pass(i, carry):
            a, b, _ = pair_of(i)
            for h in range(kv):
                values = jnp.concatenate([v_heads[h, a], v_heads[h, b]], axis=0)
                peak = top[h]
                left = jnp.exp2((scores[h, i, :, :block_tokens] - peak) * scale)
                right = jnp.exp2((scores[h, i, :, block_tokens:] - peak) * scale)
                sums[h] += left + right
                p = jnp.concatenate([left.astype(BF16), right.astype(BF16)], axis=1)
                acc[h] += jnp.dot(p, values, preferred_element_type=F32)
            return carry

        if j == 0:
            pl.when(chunk == 0)(fetch_v.wait)
        lax.fori_loop(0, pairs, second_pass, 0)
        for h in range(kv):
            half, combo = h // (kv // 2), (h % (kv // 2)) * cands + j
            total = jnp.sum(sums[h], axis=1, keepdims=True)
            stats[half] = jnp.where(lanes == combo, top[h], stats[half])
            stats[half] = jnp.where(lanes == 64 + combo, total, stats[half])
            out_ref[:, half, combo * per : (combo + 1) * per, :] = (
                acc[h].reshape(tile_owners, per, head).astype(BF16)
            )
    full = kv // 2 * cands * per
    for half in range(2):
        out_ref[:, half, full : full + per, :] = (
            stats[half].reshape(tile_owners, per, 128).astype(BF16)
        )


def merge(pieces, combos, per, scale):
    full = combos * per
    stats = [load(full, per).astype(F32) for load in pieces]
    peak = functools.reduce(jnp.maximum, stats)
    low = lax.broadcasted_iota(jnp.int32, (per, 128), 1) < 64
    scales = [jnp.exp2((jnp.where(low, s - peak, 0.0)) * scale) for s in stats]
    total = sum(pltpu.roll(w, 64, 1) * s for w, s in zip(scales, stats))
    sums = []
    for c in range(combos):
        sums.append(
            sum(
                load(c * per, per).astype(F32) * w[:, c : c + 1]
                for load, w in zip(pieces, scales)
            )
        )
    return sums, jnp.where(low, peak, total), total


def finish_kernel(
    ranges,
    sizes,
    parts_ref,
    weight_ref,
    out_ref,
    from_diag,
    from_x,
    from_y,
    from_line,
    to_diag,
    to_line,
    gathered,
    ordered,
    weight,
    total,
    away,
    arrived,
    lines,
    weight_sem,
    red_send,
    red_recv,
    send,
    recv,
    tp_sems,
):
    cands, toks, kv, group, head = sizes
    place = Place(ranges)
    depth = place.depth
    per = toks * group
    combos = kv // 2 * cands
    scale = head ** (-0.5) * math.log2(math.e)
    fetch = pltpu.make_async_copy(weight_ref, weight, weight_sem)
    fetch.start()
    greet(place, True)

    sent = []

    def copy(kind, d, half, src, dst, target):
        return pltpu.make_async_remote_copy(
            src_ref=src,
            dst_ref=dst.at[d, half],
            send_sem=red_send.at[kind, d, half],
            recv_sem=red_recv.at[kind, d, half],
            device_id={"ctx": target},
            device_id_type=MESH,
        )

    def go(*what):
        one = copy(*what)
        one.start()
        sent.append(one)

    def arrive(kind, d, half, dst):
        copy(kind, d, half, dst.at[d, half], dst, place.me).wait_recv()

    def owner(d, flip_y, flip_x):
        y = 1 - place.y if flip_y else place.y
        x = 1 - place.x if flip_x else place.x
        return place.at(place.shifted(d), y, x)

    def loader(ref, *index):
        return lambda start, size: ref[(*index, pl.ds(start, size), slice(None))]

    def put(dst, d, half, sums, stats):
        for c in range(combos):
            dst[d, half, c * per : (c + 1) * per, :] = sums[c].astype(BF16)
        dst[d, half, combos * per : (combos + 1) * per, :] = stats.astype(BF16)

    def begin(d):
        go(0, d, 0, parts_ref.at[owner(d, 1, 1), 0], from_diag, place.beside_x)
        go(0, d, 1, parts_ref.at[owner(d, 1, 1), 1], from_diag, place.beside_y)
        go(1, d, 0, parts_ref.at[owner(d, 0, 1), 0], from_x, place.beside_x)
        go(2, d, 1, parts_ref.at[owner(d, 1, 0), 1], from_y, place.beside_y)

    def pass_on(d):
        for half in range(2):
            arrive(0, d, half, from_diag)
            mine = owner(d, 1, 0) if half == 0 else owner(d, 0, 1)
            pieces = (loader(parts_ref, mine, half), loader(from_diag, d, half))
            sums, stats, _ = merge(pieces, combos, per, scale)
            put(to_diag, d, half, sums, stats)
            if half == 0:
                go(2, d, half, to_diag.at[d, half], from_y, place.beside_y)
            else:
                go(1, d, half, to_diag.at[d, half], from_x, place.beside_x)

    def plane(d):
        for half in range(2):
            arrive(1, d, half, from_x)
            arrive(2, d, half, from_y)
            pieces = (
                loader(parts_ref, owner(d, 0, 0), half),
                loader(from_x, d, half),
                loader(from_y, d, half),
            )
            sums, stats, _ = merge(pieces, combos, per, scale)
            put(to_line, d, half, sums, stats)
            if d:
                go(3, d, half, to_line.at[d, half], from_line, place.line(d))

    order = near_first(depth)[::-1] + [0]
    begin(order[0])
    begin(order[1])
    for i, d in enumerate(order):
        pass_on(d)
        if i + 2 < depth:
            begin(order[i + 2])
        if i >= 1:
            plane(order[i - 1])
    plane(order[-1])
    for half in range(2):
        for d in range(1, depth):
            arrive(3, d, half, from_line)
        sums, _, denominator = merge(
            [loader(to_line, 0, half)] + [loader(from_line, d, half) for d in range(1, depth)],
            combos,
            per,
            scale,
        )
        denominator = pltpu.roll(denominator, 64, 1)
        for c in range(combos):
            row = (half * combos + c) * per
            ordered[row : row + per, :] = sums[c] / denominator[:, c : c + 1]
    tokens = cands * toks
    for h in range(kv):
        block = [
            ordered[pl.ds(h * tokens * group + g, tokens, stride=group), :] for g in range(group)
        ]
        half, at = h // (kv // 2), (h % (kv // 2)) * tokens * group
        gathered[place.me, half, at : at + tokens * group, :] = jnp.concatenate(
            block, axis=0
        ).astype(BF16)
    gather_pieces(place, gathered, send, recv)
    fetch.wait()
    total[...] = jnp.zeros_like(total)

    def project(i, carry):
        steps = kv * group // 4
        start = pl.multiple_of((i % steps) * 2 * tokens, 2 * tokens)
        both = gathered[:, i // steps, pl.ds(start, 2 * tokens), :].astype(F32)
        left = both[:, :tokens, :].reshape(ranges * tokens, head).astype(BF16)
        right = both[:, tokens:, :].reshape(ranges * tokens, head).astype(BF16)
        rows = pl.multiple_of(i * 2 * head, 2 * head)
        total[...] += jnp.dot(
            jnp.concatenate([left, right], axis=1),
            weight[pl.ds(rows, 2 * head), :],
            preferred_element_type=F32,
        )
        return carry

    lax.fori_loop(0, kv * group // 2, project, 0)
    half = ranges * tokens // 2
    tp = lax.axis_index("tp")
    away[...] = total[pl.ds(pl.multiple_of((1 - tp) * half, half), half), :].astype(BF16)
    swap = pltpu.make_async_remote_copy(
        src_ref=away,
        dst_ref=arrived,
        send_sem=tp_sems.at[0],
        recv_sem=tp_sems.at[1],
        device_id={"tp": 1 - tp},
        device_id_type=MESH,
    )
    swap.start()
    for one in sent:
        one.wait_send()
    swap.wait()
    mine = total[pl.ds(pl.multiple_of(tp * half, half), half), :]
    columns = total.shape[1]
    joined = mine + arrived[...].astype(F32)
    owners, size = ranges // 2, ranges // 2 * toks
    for c in range(columns // 128):
        lines[c, 0] = joined[:, c * 128 : (c + 1) * 128]
        for j in range(cands):
            for t in range(toks):
                lines[c, 1, pl.ds(j * size + t, owners, stride=toks), :] = lines[
                    c, 0, pl.ds(j * toks + t, owners, stride=tokens), :
                ]
            out_ref[j, :, c * 128 : (c + 1) * 128] = lines[
                c, 1, j * size : (j + 1) * size, :
            ].astype(BF16)


def on_device(
    queries,
    cand_keys,
    candidate_values,
    cached_prompt_keys,
    cached_prompt_values,
    block_lists,
    out_weight,
):
    cands, toks, heads, head = queries.shape
    kv = cand_keys.shape[2]
    group = heads // kv
    blocks, block_tokens = cached_prompt_keys.shape[:2]
    ranges = lax.axis_size("ctx")
    depth = ranges // 4
    piece = cands * toks * heads
    per = toks * group
    vmem = pl.BlockSpec(memory_space=pltpu.VMEM)
    limit = 60 * 1024 * 1024

    anywhere = pl.BlockSpec(memory_space=pl.ANY)
    semaphores = [pltpu.SemaphoreType.DMA((4, depth, 2))] * 2
    cache = (blocks, block_tokens * kv, head)
    sorted_cache = (kv, blocks, block_tokens, head)
    everyone, keys, values = pl.pallas_call(
        functools.partial(query_kernel, ranges, kv),
        out_shape=(
            jax.ShapeDtypeStruct((ranges, 2, piece // 2, head), BF16),
            jax.ShapeDtypeStruct(sorted_cache, BF16),
            jax.ShapeDtypeStruct(sorted_cache, BF16),
        ),
        in_specs=[vmem, anywhere, anywhere],
        out_specs=(vmem, anywhere, anywhere),
        scratch_shapes=[
            pltpu.VMEM((2, *cache), BF16),
            pltpu.VMEM((block_tokens * kv, head), F32),
            pltpu.VMEM((2, *sorted_cache), BF16),
            *semaphores,
            pltpu.SemaphoreType.DMA((2,)),
            pltpu.SemaphoreType.DMA((2, 4)),
        ],
        compiler_params=pltpu.CompilerParams(
            collective_id=0, has_side_effects=True, vmem_limit_bytes=limit
        ),
        name="query_gather",
    )(
        queries.reshape(2, piece // 2, head),
        cached_prompt_keys.reshape(cache),
        cached_prompt_values.reshape(cache),
    )

    tile_owners = min(ranges, 256 // per)
    rows = tile_owners * per
    half_rows = piece // 2 + per
    whole = lambda shape: pl.BlockSpec(
        shape, lambda i, *_: (0,) * len(shape), pipeline_mode=pl.Buffered(1)
    )
    own_spec = whole(cand_keys.shape)
    sizes = (cands, toks, kv, group, blocks, block_tokens, head, tile_owners)
    parts = pl.pallas_call(
        functools.partial(attend_kernel, sizes),
        out_shape=jax.ShapeDtypeStruct((ranges, 2, half_rows, head), BF16),
        grid_spec=pltpu.PrefetchScalarGridSpec(
            num_scalar_prefetch=1,
            grid=(ranges // tile_owners,),
            in_specs=[
                whole(block_lists.shape),
                pl.BlockSpec(
                    (tile_owners, cands, toks, heads, head), lambda i, *_: (i, 0, 0, 0, 0)
                ),
                own_spec,
                own_spec,
                anywhere,
                anywhere,
            ],
            out_specs=pl.BlockSpec((tile_owners, 2, half_rows, head), lambda i, *_: (i, 0, 0, 0)),
            scratch_shapes=[
                pltpu.VMEM((kv, blocks, block_tokens, head), BF16),
                pltpu.VMEM((kv, blocks, block_tokens, head), BF16),
                pltpu.VMEM((kv, (blocks + 1) // 2, rows, 2 * block_tokens), F32),
                pltpu.VMEM((kv, rows, block_tokens), F32),
                pltpu.VMEM((kv, rows, head), F32),
                pltpu.VMEM((kv, rows, block_tokens), F32),
                pltpu.SemaphoreType.DMA((2,)),
            ],
        ),
        compiler_params=pltpu.CompilerParams(vmem_limit_bytes=limit),
        name="attend",
    )(
        block_lists,
        block_lists,
        everyone.reshape(ranges, cands, toks, heads, head),
        cand_keys,
        candidate_values,
        keys,
        values,
    )

    columns = out_weight.shape[1]
    tokens = cands * toks
    half = ranges * tokens // 2
    block = pltpu.VMEM((depth, 2, half_rows, head), BF16)
    return pl.pallas_call(
        functools.partial(finish_kernel, ranges, (cands, toks, kv, group, head)),
        out_shape=jax.ShapeDtypeStruct((cands, ranges * toks // 2, columns), BF16),
        in_specs=[vmem, pl.BlockSpec(memory_space=pl.ANY)],
        out_specs=vmem,
        scratch_shapes=[block] * 6
        + [
            pltpu.VMEM((ranges, 2, piece // 2, head), BF16),
            pltpu.VMEM((piece, head), F32),
            pltpu.VMEM(out_weight.shape, BF16),
            pltpu.VMEM((2 * half, columns), F32),
            pltpu.VMEM((half, columns), BF16),
            pltpu.VMEM((half, columns), BF16),
            pltpu.VMEM((columns // 128, 2, half, 128), F32),
            pltpu.SemaphoreType.DMA,
            *semaphores,
            *semaphores,
            pltpu.SemaphoreType.DMA((2,)),
        ],
        compiler_params=pltpu.CompilerParams(
            collective_id=1, has_side_effects=True, vmem_limit_bytes=limit
        ),
        name="reduce_project",
    )(parts, out_weight)


def solution(mesh):
    placed = (
        P("groups", "ctx", "tp", None),
        P("groups", "ctx", "tp", None),
        P("groups", "ctx", "tp", None),
        P(("groups", "ctx"), None, "tp", None),
        P(("groups", "ctx"), None, "tp", None),
        P("groups", None),
        P("tp", "ctx"),
    )
    return jax.shard_map(
        on_device, mesh=mesh, in_specs=placed, out_specs=P("groups", "tp", "ctx"), check_vma=False
    )
```

```python
import functools
import math

import jax
import jax.numpy as jnp
from jax import lax
from jax.experimental import pallas as pl
from jax.experimental.pallas import tpu as pltpu
from jax.sharding import PartitionSpec as P

NEGATIVE = -1e30
MESH = pl.DeviceIdType.MESH
F32, BF16 = jnp.float32, jnp.bfloat16


class Place:
    def __init__(self, ranges):
        self.me = lax.axis_index("ctx")
        self.depth = ranges // 4
        self.x, self.y, self.z = self.me % 2, (self.me // 2) % 2, self.me // 4
        self.beside_x = self.at(self.z, self.y, 1 - self.x)
        self.beside_y = self.at(self.z, 1 - self.y, self.x)

    def at(self, z, y, x):
        return z * 4 + y * 2 + x

    def shifted(self, d):
        return (self.z + d + self.depth) % self.depth

    def line(self, d):
        return self.at(self.shifted(d), self.y, self.x)


def greet(place, with_tp):
    barrier = pltpu.get_barrier_semaphore()
    others = [place.line(d) for d in range(1, place.depth)]
    for other in others + [place.beside_x, place.beside_y]:
        pl.semaphore_signal(barrier, inc=1, device_id={"ctx": other}, device_id_type=MESH)
    if with_tp:
        pl.semaphore_signal(
            barrier, inc=1, device_id={"tp": 1 - lax.axis_index("tp")}, device_id_type=MESH
        )
    pl.semaphore_wait(barrier, place.depth + 1 + int(with_tp))


def near_first(depth):
    order = []
    for step in range(1, depth // 2 + 1):
        order += [step] + ([depth - step] if depth - step != step else [])
    return order


def gather_pieces(place, buf, send, recv, work=lambda step: None):
    def copy(kind, d, half, owner, target):
        return pltpu.make_async_remote_copy(
            src_ref=buf.at[owner, half],
            dst_ref=buf.at[owner, half],
            send_sem=send.at[kind, d, half],
            recv_sem=recv.at[kind, d, half],
            device_id={"ctx": target},
            device_id_type=MESH,
        )

    sent = []

    def go(*what):
        one = copy(*what)
        one.start()
        sent.append(one)

    depth = place.depth
    z_of = [place.shifted(-d) for d in range(depth)]

    def spread(d, half):
        owner = place.at(z_of[d], place.y, place.x)
        if d:
            copy(0, d, half, owner, place.me).wait_recv()
        go(1, d, half, owner, place.beside_x)
        go(2, d, half, owner, place.beside_y)

    def relay(d, half):
        from_x = place.at(z_of[d], place.y, 1 - place.x)
        from_y = place.at(z_of[d], 1 - place.y, place.x)
        if half == 0:
            copy(1, d, half, from_x, place.me).wait_recv()
            go(3, d, half, from_x, place.beside_y)
        else:
            copy(2, d, half, from_y, place.me).wait_recv()
            go(3, d, half, from_y, place.beside_x)

    def settle(d, half):
        from_x = place.at(z_of[d], place.y, 1 - place.x)
        from_y = place.at(z_of[d], 1 - place.y, place.x)
        if half == 0:
            copy(2, d, half, from_y, place.me).wait_recv()
        else:
            copy(1, d, half, from_x, place.me).wait_recv()
        across = place.at(z_of[d], 1 - place.y, 1 - place.x)
        copy(3, d, half, across, place.me).wait_recv()

    order = near_first(depth)
    for half in range(2):
        spread(0, half)
    for d in order:
        for half in range(2):
            go(0, d, half, place.me, place.line(d))
    work(0)
    steps = [(d, half) for d in [0] + order for half in range(2)]
    for i, step in enumerate(steps):
        if i + 2 < len(steps):
            spread(*steps[i + 2])
        relay(*step)
        work(i + 1)
    for step in steps:
        settle(*step)
    for one in sent:
        one.wait_send()


def query_kernel(
    ranges,
    kv,
    q_ref,
    k_ref,
    v_ref,
    out_ref,
    k_out,
    v_out,
    raw,
    wide,
    heads,
    send,
    recv,
    in_sems,
    out_sems,
):
    place = Place(ranges)
    sources, results = (k_ref, v_ref), (k_out, v_out)
    fetches = [pltpu.make_async_copy(sources[n], raw.at[n], in_sems.at[n]) for n in range(2)]
    for fetch in fetches:
        fetch.start()
    out_ref[place.me] = q_ref[...]
    greet(place, False)
    blocks, block_tokens = raw.shape[1], raw.shape[2] // kv
    parts = 4
    per = blocks // parts
    stores = []

    def work(step):
        if step >= 2 * parts:
            return
        n, part = step // parts, step % parts
        if part == 0:
            fetches[n].wait()

        def one(b, carry):
            wide[...] = raw[n, b].astype(F32)
            for h in range(kv):
                heads[n, h, b] = wide[pl.ds(h, block_tokens, stride=kv), :].astype(BF16)
            return carry

        lax.fori_loop(part * per, (part + 1) * per, one, 0)
        some = pl.ds(part * per, per)
        store = pltpu.make_async_copy(
            heads.at[n, :, some], results[n].at[:, some], out_sems.at[n, part]
        )
        store.start()
        stores.append(store)

    gather_pieces(place, out_ref, send, recv, work)
    for store in stores:
        store.wait()


def attend_kernel(
    sizes,
    lists_smem,
    lists_ref,
    q_ref,
    own_k_ref,
    own_v_ref,
    k_ref,
    v_ref,
    out_ref,
    k_heads,
    v_heads,
    scores,
    sums,
    acc,
    top,
    sems,
):
    cands, toks, kv, group, blocks, block_tokens, head, tile_owners = sizes
    chunk = pl.program_id(0)
    me = lax.axis_index("ctx")
    scale = head ** (-0.5) * math.log2(math.e)
    rows = tile_owners * toks * group
    lowest = me * blocks

    fetch_k = pltpu.make_async_copy(k_ref, k_heads, sems.at[0])
    fetch_v = pltpu.make_async_copy(v_ref, v_heads, sems.at[1])

    @pl.when(chunk == 0)
    def _():
        fetch_k.start()
        fetch_v.start()

    key_row = lax.broadcasted_iota(jnp.int32, (block_tokens, head), 0)

    def own_block(ref, h, j):
        rows_here = ref[j].astype(F32)
        block = jnp.zeros((block_tokens, head), F32)
        for t in range(toks):
            block = jnp.where(key_row == t, rows_here[t, h : h + 1, :], block)
        return block.astype(BF16)

    row = lax.broadcasted_iota(jnp.int32, (rows, block_tokens), 0)
    lane = lax.broadcasted_iota(jnp.int32, (rows, block_tokens), 1)
    query_pos = chunk * tile_owners * toks + row // group
    own_seen = (lane < toks) & (me * toks + lane <= query_pos)
    stats = [jnp.zeros((rows, 128), F32)] * 2
    per = toks * group
    lanes = lax.broadcasted_iota(jnp.int32, (rows, 128), 1)
    nt = (((1,), (1,)), ((), ()))
    for j in range(cands):
        line = lists_ref[j : j + 1, :]
        below = jnp.sum((line < lowest).astype(jnp.int32))
        count = jnp.sum((line < lowest + blocks).astype(jnp.int32)) - below
        last = lists_smem.shape[1] - 1

        def listed(slot):
            return lists_smem[j, jnp.minimum(below + slot, last)] - lowest

        fours = count // 4
        pairs = (count - 4 * fours + 1) // 2

        def four_of(i):
            return 4 * i, [listed(4 * i + n) for n in range(4)], None

        def pair_of(i):
            slot = 4 * fours + 2 * i
            inside = slot + 1 < count
            first = listed(slot)
            return slot, [first, jnp.where(inside, listed(slot + 1), first)], inside

        def scores_of(h, picked):
            keys = jnp.concatenate([k_heads[h, b] for b in picked], axis=0)
            s = lax.dot_general(queries[h], keys, nt, preferred_element_type=F32)
            return [s[:, n * block_tokens : (n + 1) * block_tokens] for n in range(len(picked))]

        queries = []
        for h in range(kv):
            q = q_ref[:, j, :, h * group : (h + 1) * group, :].astype(F32)
            queries.append(q.reshape(rows, head).astype(BF16))
            own = lax.dot_general(
                queries[h], own_block(own_k_ref, h, j), nt, preferred_element_type=F32
            )
            own = jnp.where(own_seen, own, NEGATIVE)
            sums[h] = own
            top[h] = own

        if j == 0:
            pl.when(chunk == 0)(fetch_k.wait)

        def first_pass(pick, i, carry):
            slot, picked, _ = pick(i)
            for h in range(kv):
                found = scores_of(h, picked)
                for n, s in enumerate(found):
                    scores[h, slot + n] = s
                top[h] = functools.reduce(jnp.maximum, found, top[h])
            return carry

        lax.fori_loop(0, fours, functools.partial(first_pass, four_of), 0)
        lax.fori_loop(0, pairs, functools.partial(first_pass, pair_of), 0)
        for h in range(kv):
            peak = jnp.max(top[h], axis=1, keepdims=True).astype(BF16).astype(F32)
            p = jnp.where(own_seen, jnp.exp2((sums[h] - peak) * scale), 0.0)
            sums[h] = p
            acc[h] = jnp.dot(
                p.astype(BF16), own_block(own_v_ref, h, j), preferred_element_type=F32
            )
            top[h] = jnp.broadcast_to(peak, (rows, block_tokens))

        def second_pass(pick, i, carry):
            slot, picked, inside = pick(i)
            for h in range(kv):
                peak = top[h]
                p = [
                    jnp.exp2((scores[h, slot + n] - peak) * scale) for n in range(len(picked))
                ]
                if inside is not None:
                    p[-1] = jnp.where(inside, p[-1], 0.0)
                sums[h] += functools.reduce(jnp.add, p)
                values = jnp.concatenate([v_heads[h, b] for b in picked], axis=0)
                weights = jnp.concatenate([one.astype(BF16) for one in p], axis=1)
                acc[h] += jnp.dot(weights, values, preferred_element_type=F32)
            return carry

        if j == 0:
            pl.when(chunk == 0)(fetch_v.wait)
        lax.fori_loop(0, fours, functools.partial(second_pass, four_of), 0)
        lax.fori_loop(0, pairs, functools.partial(second_pass, pair_of), 0)
        for h in range(kv):
            half, combo = h // (kv // 2), (h % (kv // 2)) * cands + j
            total = jnp.sum(sums[h], axis=1, keepdims=True)
            stats[half] = jnp.where(lanes == combo, top[h], stats[half])
            stats[half] = jnp.where(lanes == 64 + combo, total, stats[half])
            out_ref[:, half, combo * per : (combo + 1) * per, :] = (
                acc[h].reshape(tile_owners, per, head).astype(BF16)
            )
    full = kv // 2 * cands * per
    for half in range(2):
        out_ref[:, half, full : full + per, :] = (
            stats[half].reshape(tile_owners, per, 128).astype(BF16)
        )


def merge(pieces, combos, per, scale):
    full = combos * per
    stats = [load(full, per).astype(F32) for load in pieces]
    peak = functools.reduce(jnp.maximum, stats)
    low = lax.broadcasted_iota(jnp.int32, (per, 128), 1) < 64
    scales = [jnp.exp2((jnp.where(low, s - peak, 0.0)) * scale) for s in stats]
    total = sum(pltpu.roll(w, 64, 1) * s for w, s in zip(scales, stats))
    sums = []
    for c in range(combos):
        sums.append(
            sum(
                load(c * per, per).astype(F32) * w[:, c : c + 1]
                for load, w in zip(pieces, scales)
            )
        )
    return sums, jnp.where(low, peak, total), total


def finish_kernel(
    ranges,
    sizes,
    parts_ref,
    weight_ref,
    out_ref,
    from_diag,
    from_x,
    from_y,
    from_line,
    to_diag,
    to_line,
    gathered,
    ordered,
    weight,
    total,
    away,
    arrived,
    lines,
    weight_sem,
    red_send,
    red_recv,
    send,
    recv,
    tp_sems,
):
    cands, toks, kv, group, head = sizes
    place = Place(ranges)
    depth = place.depth
    per = toks * group
    combos = kv // 2 * cands
    scale = head ** (-0.5) * math.log2(math.e)
    fetch = pltpu.make_async_copy(weight_ref, weight, weight_sem)
    fetch.start()
    greet(place, True)

    sent = []

    def copy(kind, d, half, src, dst, target):
        return pltpu.make_async_remote_copy(
            src_ref=src,
            dst_ref=dst.at[d, half],
            send_sem=red_send.at[kind, d, half],
            recv_sem=red_recv.at[kind, d, half],
            device_id={"ctx": target},
            device_id_type=MESH,
        )

    def go(*what):
        one = copy(*what)
        one.start()
        sent.append(one)

    def arrive(kind, d, half, dst):
        copy(kind, d, half, dst.at[d, half], dst, place.me).wait_recv()

    def owner(d, flip_y, flip_x):
        y = 1 - place.y if flip_y else place.y
        x = 1 - place.x if flip_x else place.x
        return place.at(place.shifted(d), y, x)

    def loader(ref, *index):
        return lambda start, size: ref[(*index, pl.ds(start, size), slice(None))]

    def put(dst, d, half, sums, stats):
        for c in range(combos):
            dst[d, half, c * per : (c + 1) * per, :] = sums[c].astype(BF16)
        dst[d, half, combos * per : (combos + 1) * per, :] = stats.astype(BF16)

    def begin(d):
        go(0, d, 0, parts_ref.at[owner(d, 1, 1), 0], from_diag, place.beside_x)
        go(0, d, 1, parts_ref.at[owner(d, 1, 1), 1], from_diag, place.beside_y)
        go(1, d, 0, parts_ref.at[owner(d, 0, 1), 0], from_x, place.beside_x)
        go(2, d, 1, parts_ref.at[owner(d, 1, 0), 1], from_y, place.beside_y)

    def pass_on(d):
        for half in range(2):
            arrive(0, d, half, from_diag)
            mine = owner(d, 1, 0) if half == 0 else owner(d, 0, 1)
            pieces = (loader(parts_ref, mine, half), loader(from_diag, d, half))
            sums, stats, _ = merge(pieces, combos, per, scale)
            put(to_diag, d, half, sums, stats)
            if half == 0:
                go(2, d, half, to_diag.at[d, half], from_y, place.beside_y)
            else:
                go(1, d, half, to_diag.at[d, half], from_x, place.beside_x)

    def plane(d):
        for half in range(2):
            arrive(1, d, half, from_x)
            arrive(2, d, half, from_y)
            pieces = (
                loader(parts_ref, owner(d, 0, 0), half),
                loader(from_x, d, half),
                loader(from_y, d, half),
            )
            sums, stats, _ = merge(pieces, combos, per, scale)
            put(to_line, d, half, sums, stats)
            if d:
                go(3, d, half, to_line.at[d, half], from_line, place.line(d))

    order = near_first(depth)[::-1] + [0]
    begin(order[0])
    begin(order[1])
    for i, d in enumerate(order):
        pass_on(d)
        if i + 2 < depth:
            begin(order[i + 2])
        if i >= 1:
            plane(order[i - 1])
    plane(order[-1])
    for half in range(2):
        for d in range(1, depth):
            arrive(3, d, half, from_line)
        sums, _, denominator = merge(
            [loader(to_line, 0, half)] + [loader(from_line, d, half) for d in range(1, depth)],
            combos,
            per,
            scale,
        )
        denominator = pltpu.roll(denominator, 64, 1)
        for c in range(combos):
            row = (half * combos + c) * per
            ordered[row : row + per, :] = sums[c] / denominator[:, c : c + 1]
    tokens = cands * toks
    for h in range(kv):
        block = [
            ordered[pl.ds(h * tokens * group + g, tokens, stride=group), :] for g in range(group)
        ]
        half, at = h // (kv // 2), (h % (kv // 2)) * tokens * group
        gathered[place.me, half, at : at + tokens * group, :] = jnp.concatenate(
            block, axis=0
        ).astype(BF16)
    gather_pieces(place, gathered, send, recv)
    fetch.wait()
    total[...] = jnp.zeros_like(total)

    def project(i, carry):
        steps = kv * group // 4
        start = pl.multiple_of((i % steps) * 2 * tokens, 2 * tokens)
        both = gathered[:, i // steps, pl.ds(start, 2 * tokens), :].astype(F32)
        left = both[:, :tokens, :].reshape(ranges * tokens, head).astype(BF16)
        right = both[:, tokens:, :].reshape(ranges * tokens, head).astype(BF16)
        rows = pl.multiple_of(i * 2 * head, 2 * head)
        total[...] += jnp.dot(
            jnp.concatenate([left, right], axis=1),
            weight[pl.ds(rows, 2 * head), :],
            preferred_element_type=F32,
        )
        return carry

    lax.fori_loop(0, kv * group // 2, project, 0)
    half = ranges * tokens // 2
    tp = lax.axis_index("tp")
    away[...] = total[pl.ds(pl.multiple_of((1 - tp) * half, half), half), :].astype(BF16)
    swap = pltpu.make_async_remote_copy(
        src_ref=away,
        dst_ref=arrived,
        send_sem=tp_sems.at[0],
        recv_sem=tp_sems.at[1],
        device_id={"tp": 1 - tp},
        device_id_type=MESH,
    )
    swap.start()
    for one in sent:
        one.wait_send()
    swap.wait()
    mine = total[pl.ds(pl.multiple_of(tp * half, half), half), :]
    columns = total.shape[1]
    joined = mine + arrived[...].astype(F32)
    owners, size = ranges // 2, ranges // 2 * toks
    for c in range(columns // 128):
        lines[c, 0] = joined[:, c * 128 : (c + 1) * 128]
        for j in range(cands):
            for t in range(toks):
                lines[c, 1, pl.ds(j * size + t, owners, stride=toks), :] = lines[
                    c, 0, pl.ds(j * toks + t, owners, stride=tokens), :
                ]
            out_ref[j, :, c * 128 : (c + 1) * 128] = lines[
                c, 1, j * size : (j + 1) * size, :
            ].astype(BF16)


def on_device(
    queries,
    cand_keys,
    candidate_values,
    cached_prompt_keys,
    cached_prompt_values,
    block_lists,
    out_weight,
):
    cands, toks, heads, head = queries.shape
    kv = cand_keys.shape[2]
    group = heads // kv
    blocks, block_tokens = cached_prompt_keys.shape[:2]
    ranges = lax.axis_size("ctx")
    depth = ranges // 4
    piece = cands * toks * heads
    per = toks * group
    vmem = pl.BlockSpec(memory_space=pltpu.VMEM)
    limit = 60 * 1024 * 1024

    anywhere = pl.BlockSpec(memory_space=pl.ANY)
    semaphores = [pltpu.SemaphoreType.DMA((4, depth, 2))] * 2
    cache = (blocks, block_tokens * kv, head)
    sorted_cache = (kv, blocks, block_tokens, head)
    everyone, keys, values = pl.pallas_call(
        functools.partial(query_kernel, ranges, kv),
        out_shape=(
            jax.ShapeDtypeStruct((ranges, 2, piece // 2, head), BF16),
            jax.ShapeDtypeStruct(sorted_cache, BF16),
            jax.ShapeDtypeStruct(sorted_cache, BF16),
        ),
        in_specs=[vmem, anywhere, anywhere],
        out_specs=(vmem, anywhere, anywhere),
        scratch_shapes=[
            pltpu.VMEM((2, *cache), BF16),
            pltpu.VMEM((block_tokens * kv, head), F32),
            pltpu.VMEM((2, *sorted_cache), BF16),
            *semaphores,
            pltpu.SemaphoreType.DMA((2,)),
            pltpu.SemaphoreType.DMA((2, 4)),
        ],
        compiler_params=pltpu.CompilerParams(
            collective_id=0, has_side_effects=True, vmem_limit_bytes=limit
        ),
        name="query_gather",
    )(
        queries.reshape(2, piece // 2, head),
        cached_prompt_keys.reshape(cache),
        cached_prompt_values.reshape(cache),
    )

    tile_owners = min(ranges, 256 // per)
    rows = tile_owners * per
    half_rows = piece // 2 + per
    whole = lambda shape: pl.BlockSpec(
        shape, lambda i, *_: (0,) * len(shape), pipeline_mode=pl.Buffered(1)
    )
    own_spec = whole(cand_keys.shape)
    sizes = (cands, toks, kv, group, blocks, block_tokens, head, tile_owners)
    parts = pl.pallas_call(
        functools.partial(attend_kernel, sizes),
        out_shape=jax.ShapeDtypeStruct((ranges, 2, half_rows, head), BF16),
        grid_spec=pltpu.PrefetchScalarGridSpec(
            num_scalar_prefetch=1,
            grid=(ranges // tile_owners,),
            in_specs=[
                whole(block_lists.shape),
                pl.BlockSpec(
                    (tile_owners, cands, toks, heads, head), lambda i, *_: (i, 0, 0, 0, 0)
                ),
                own_spec,
                own_spec,
                anywhere,
                anywhere,
            ],
            out_specs=pl.BlockSpec((tile_owners, 2, half_rows, head), lambda i, *_: (i, 0, 0, 0)),
            scratch_shapes=[
                pltpu.VMEM((kv, blocks, block_tokens, head), BF16),
                pltpu.VMEM((kv, blocks, block_tokens, head), BF16),
                pltpu.VMEM((kv, (blocks + 1) // 2 * 2, rows, block_tokens), F32),
                pltpu.VMEM((kv, rows, block_tokens), F32),
                pltpu.VMEM((kv, rows, head), F32),
                pltpu.VMEM((kv, rows, block_tokens), F32),
                pltpu.SemaphoreType.DMA((2,)),
            ],
        ),
        compiler_params=pltpu.CompilerParams(vmem_limit_bytes=limit),
        name="attend",
    )(
        block_lists,
        block_lists,
        everyone.reshape(ranges, cands, toks, heads, head),
        cand_keys,
        candidate_values,
        keys,
        values,
    )

    columns = out_weight.shape[1]
    tokens = cands * toks
    half = ranges * tokens // 2
    block = pltpu.VMEM((depth, 2, half_rows, head), BF16)
    return pl.pallas_call(
        functools.partial(finish_kernel, ranges, (cands, toks, kv, group, head)),
        out_shape=jax.ShapeDtypeStruct((cands, ranges * toks // 2, columns), BF16),
        in_specs=[vmem, pl.BlockSpec(memory_space=pl.ANY)],
        out_specs=vmem,
        scratch_shapes=[block] * 6
        + [
            pltpu.VMEM((ranges, 2, piece // 2, head), BF16),
            pltpu.VMEM((piece, head), F32),
            pltpu.VMEM(out_weight.shape, BF16),
            pltpu.VMEM((2 * half, columns), F32),
            pltpu.VMEM((half, columns), BF16),
            pltpu.VMEM((half, columns), BF16),
            pltpu.VMEM((columns // 128, 2, half, 128), F32),
            pltpu.SemaphoreType.DMA,
            *semaphores,
            *semaphores,
            pltpu.SemaphoreType.DMA((2,)),
        ],
        compiler_params=pltpu.CompilerParams(
            collective_id=1, has_side_effects=True, vmem_limit_bytes=limit
        ),
        name="reduce_project",
    )(parts, out_weight)


def solution(mesh):
    placed = (
        P("groups", "ctx", "tp", None),
        P("groups", "ctx", "tp", None),
        P("groups", "ctx", "tp", None),
        P(("groups", "ctx"), None, "tp", None),
        P(("groups", "ctx"), None, "tp", None),
        P("groups", None),
        P("tp", "ctx"),
    )
    return jax.shard_map(
        on_device, mesh=mesh, in_specs=placed, out_specs=P("groups", "tp", "ctx"), check_vma=False
    )
```

```python
import functools
import math

import jax
import jax.numpy as jnp
from jax import lax
from jax.experimental import pallas as pl
from jax.experimental.pallas import tpu as pltpu
from jax.sharding import PartitionSpec as P

NEGATIVE = -1e30
MESH = pl.DeviceIdType.MESH
F32, BF16 = jnp.float32, jnp.bfloat16


class Place:
    def __init__(self, ranges):
        self.me = lax.axis_index("ctx")
        self.depth = ranges // 4
        self.x, self.y, self.z = self.me % 2, (self.me // 2) % 2, self.me // 4
        self.beside_x = self.at(self.z, self.y, 1 - self.x)
        self.beside_y = self.at(self.z, 1 - self.y, self.x)

    def at(self, z, y, x):
        return z * 4 + y * 2 + x

    def shifted(self, d):
        return (self.z + d + self.depth) % self.depth

    def line(self, d):
        return self.at(self.shifted(d), self.y, self.x)


def greet(place, with_tp):
    barrier = pltpu.get_barrier_semaphore()
    others = [place.line(d) for d in range(1, place.depth)]
    for other in others + [place.beside_x, place.beside_y]:
        pl.semaphore_signal(barrier, inc=1, device_id={"ctx": other}, device_id_type=MESH)
    if with_tp:
        pl.semaphore_signal(
            barrier, inc=1, device_id={"tp": 1 - lax.axis_index("tp")}, device_id_type=MESH
        )
    pl.semaphore_wait(barrier, place.depth + 1 + int(with_tp))


def near_first(depth):
    order = []
    for step in range(1, depth // 2 + 1):
        order += [step] + ([depth - step] if depth - step != step else [])
    return order


def gather_pieces(place, buf, send, recv, prepare, work=lambda step: None):
    def copy(kind, d, half, owner, target):
        return pltpu.make_async_remote_copy(
            src_ref=buf.at[owner, half],
            dst_ref=buf.at[owner, half],
            send_sem=send.at[kind, d, half],
            recv_sem=recv.at[kind, d, half],
            device_id={"ctx": target},
            device_id_type=MESH,
        )

    sent = []

    def go(*what):
        one = copy(*what)
        one.start()
        sent.append(one)

    depth = place.depth
    z_of = [place.shifted(-d) for d in range(depth)]

    def spread(d, half):
        owner = place.at(z_of[d], place.y, place.x)
        if d:
            copy(0, d, half, owner, place.me).wait_recv()
        go(1, d, half, owner, place.beside_x)
        go(2, d, half, owner, place.beside_y)

    def relay(d, half):
        from_x = place.at(z_of[d], place.y, 1 - place.x)
        from_y = place.at(z_of[d], 1 - place.y, place.x)
        if half == 0:
            copy(1, d, half, from_x, place.me).wait_recv()
            go(3, d, half, from_x, place.beside_y)
        else:
            copy(2, d, half, from_y, place.me).wait_recv()
            go(3, d, half, from_y, place.beside_x)

    def settle(d, half):
        from_x = place.at(z_of[d], place.y, 1 - place.x)
        from_y = place.at(z_of[d], 1 - place.y, place.x)
        if half == 0:
            copy(2, d, half, from_y, place.me).wait_recv()
        else:
            copy(1, d, half, from_x, place.me).wait_recv()
        across = place.at(z_of[d], 1 - place.y, 1 - place.x)
        copy(3, d, half, across, place.me).wait_recv()

    order = near_first(depth)
    for half in range(2):
        prepare(half)
        for d in order:
            go(0, d, half, place.me, place.line(d))
        spread(0, half)
    work(0)
    steps = [(d, half) for d in [0] + order for half in range(2)]
    for i, step in enumerate(steps):
        if i + 2 < len(steps):
            spread(*steps[i + 2])
        relay(*step)
        work(i + 1)
    for step in steps:
        settle(*step)
    for one in sent:
        one.wait_send()


def query_kernel(
    ranges,
    kv,
    q_ref,
    k_ref,
    v_ref,
    out_ref,
    k_out,
    v_out,
    raw,
    wide,
    heads,
    send,
    recv,
    in_sems,
    out_sems,
):
    place = Place(ranges)
    sources, results = (k_ref, v_ref), (k_out, v_out)
    fetches = [pltpu.make_async_copy(sources[n], raw.at[n], in_sems.at[n]) for n in range(2)]
    for fetch in fetches:
        fetch.start()
    out_ref[place.me] = q_ref[...]
    greet(place, False)
    prepare = lambda half: None
    blocks, block_tokens = raw.shape[1], raw.shape[2] // kv
    parts = 4
    per = blocks // parts
    stores = []

    def work(step):
        if step >= 2 * parts:
            return
        n, part = step // parts, step % parts
        if part == 0:
            fetches[n].wait()

        def one(b, carry):
            wide[...] = raw[n, b].astype(F32)
            for h in range(kv):
                heads[n, h, b] = wide[pl.ds(h, block_tokens, stride=kv), :].astype(BF16)
            return carry

        lax.fori_loop(part * per, (part + 1) * per, one, 0)
        some = pl.ds(part * per, per)
        store = pltpu.make_async_copy(
            heads.at[n, :, some], results[n].at[:, some], out_sems.at[n, part]
        )
        store.start()
        stores.append(store)

    gather_pieces(place, out_ref, send, recv, prepare, work)
    for store in stores:
        store.wait()


def attend_kernel(
    sizes,
    lists_smem,
    lists_ref,
    q_ref,
    own_k_ref,
    own_v_ref,
    k_ref,
    v_ref,
    out_ref,
    k_heads,
    v_heads,
    scores,
    sums,
    acc,
    top,
    sems,
):
    cands, toks, kv, group, blocks, block_tokens, head, tile_owners = sizes
    chunk = pl.program_id(0)
    me = lax.axis_index("ctx")
    scale = head ** (-0.5) * math.log2(math.e)
    rows = tile_owners * toks * group
    lowest = me * blocks

    fetch_k = pltpu.make_async_copy(k_ref, k_heads, sems.at[0])
    fetch_v = pltpu.make_async_copy(v_ref, v_heads, sems.at[1])

    @pl.when(chunk == 0)
    def _():
        fetch_k.start()
        fetch_v.start()

    key_row = lax.broadcasted_iota(jnp.int32, (block_tokens, head), 0)

    def own_block(ref, h, j):
        rows_here = ref[j].astype(F32)
        block = jnp.zeros((block_tokens, head), F32)
        for t in range(toks):
            block = jnp.where(key_row == t, rows_here[t, h : h + 1, :], block)
        return block.astype(BF16)

    row = lax.broadcasted_iota(jnp.int32, (rows, block_tokens), 0)
    lane = lax.broadcasted_iota(jnp.int32, (rows, block_tokens), 1)
    query_pos = chunk * tile_owners * toks + row // group
    own_seen = (lane < toks) & (me * toks + lane <= query_pos)
    stats = [jnp.zeros((rows, 128), F32)] * 2
    per = toks * group
    lanes = lax.broadcasted_iota(jnp.int32, (rows, 128), 1)
    nt = (((1,), (1,)), ((), ()))
    for j in range(cands):
        line = lists_ref[j : j + 1, :]
        below = jnp.sum((line < lowest).astype(jnp.int32))
        count = jnp.sum((line < lowest + blocks).astype(jnp.int32)) - below
        last = lists_smem.shape[1] - 1

        def listed(slot):
            return lists_smem[j, jnp.minimum(below + slot, last)] - lowest

        fours = count // 4
        pairs = (count - 4 * fours + 1) // 2

        def four_of(i):
            return 4 * i, [listed(4 * i + n) for n in range(4)], None

        def pair_of(i):
            slot = 4 * fours + 2 * i
            inside = slot + 1 < count
            first = listed(slot)
            return slot, [first, jnp.where(inside, listed(slot + 1), first)], inside

        def scores_of(h, picked):
            keys = jnp.concatenate([k_heads[h, b] for b in picked], axis=0)
            s = lax.dot_general(queries[h], keys, nt, preferred_element_type=F32)
            return [s[:, n * block_tokens : (n + 1) * block_tokens] for n in range(len(picked))]

        queries = []
        for h in range(kv):
            q = q_ref[:, j, :, h * group : (h + 1) * group, :].astype(F32)
            queries.append(q.reshape(rows, head).astype(BF16))
            own = lax.dot_general(
                queries[h], own_block(own_k_ref, h, j), nt, preferred_element_type=F32
            )
            own = jnp.where(own_seen, own, NEGATIVE)
            sums[h] = own
            top[h] = own

        if j == 0:
            pl.when(chunk == 0)(fetch_k.wait)

        def first_pass(pick, i, carry):
            slot, picked, _ = pick(i)
            for h in range(kv):
                found = scores_of(h, picked)
                for n, s in enumerate(found):
                    scores[h, slot + n] = s
                top[h] = functools.reduce(jnp.maximum, found, top[h])
            return carry

        lax.fori_loop(0, fours, functools.partial(first_pass, four_of), 0)
        lax.fori_loop(0, pairs, functools.partial(first_pass, pair_of), 0)
        for h in range(kv):
            peak = jnp.max(top[h], axis=1, keepdims=True).astype(BF16).astype(F32)
            p = jnp.where(own_seen, jnp.exp2((sums[h] - peak) * scale), 0.0)
            sums[h] = p
            acc[h] = jnp.dot(
                p.astype(BF16), own_block(own_v_ref, h, j), preferred_element_type=F32
            )
            top[h] = jnp.broadcast_to(peak, (rows, block_tokens))

        def second_pass(pick, i, carry):
            slot, picked, inside = pick(i)
            for h in range(kv):
                peak = top[h]
                p = [
                    jnp.exp2((scores[h, slot + n] - peak) * scale) for n in range(len(picked))
                ]
                if inside is not None:
                    p[-1] = jnp.where(inside, p[-1], 0.0)
                sums[h] += functools.reduce(jnp.add, p)
                values = jnp.concatenate([v_heads[h, b] for b in picked], axis=0)
                weights = jnp.concatenate([one.astype(BF16) for one in p], axis=1)
                acc[h] += jnp.dot(weights, values, preferred_element_type=F32)
            return carry

        if j == 0:
            pl.when(chunk == 0)(fetch_v.wait)
        lax.fori_loop(0, fours, functools.partial(second_pass, four_of), 0)
        lax.fori_loop(0, pairs, functools.partial(second_pass, pair_of), 0)
        for h in range(kv):
            half, combo = h // (kv // 2), (h % (kv // 2)) * cands + j
            total = jnp.sum(sums[h], axis=1, keepdims=True)
            stats[half] = jnp.where(lanes == combo, top[h], stats[half])
            stats[half] = jnp.where(lanes == 64 + combo, total, stats[half])
            out_ref[:, half, combo * per : (combo + 1) * per, :] = (
                acc[h].reshape(tile_owners, per, head).astype(BF16)
            )
    full = kv // 2 * cands * per
    for half in range(2):
        out_ref[:, half, full : full + per, :] = (
            stats[half].reshape(tile_owners, per, 128).astype(BF16)
        )


def merge(pieces, combos, per, scale):
    full = combos * per
    stats = [load(full, per).astype(F32) for load in pieces]
    peak = functools.reduce(jnp.maximum, stats)
    low = lax.broadcasted_iota(jnp.int32, (per, 128), 1) < 64
    scales = [jnp.exp2((jnp.where(low, s - peak, 0.0)) * scale) for s in stats]
    total = sum(pltpu.roll(w, 64, 1) * s for w, s in zip(scales, stats))
    sums = []
    for c in range(combos):
        sums.append(
            sum(
                load(c * per, per).astype(F32) * w[:, c : c + 1]
                for load, w in zip(pieces, scales)
            )
        )
    return sums, jnp.where(low, peak, total), total


def finish_kernel(
    ranges,
    sizes,
    parts_ref,
    weight_ref,
    out_ref,
    from_diag,
    from_x,
    from_y,
    from_line,
    to_diag,
    to_line,
    gathered,
    ordered,
    weight,
    total,
    away,
    arrived,
    lines,
    weight_sem,
    red_send,
    red_recv,
    send,
    recv,
    tp_sems,
):
    cands, toks, kv, group, head = sizes
    place = Place(ranges)
    depth = place.depth
    per = toks * group
    combos = kv // 2 * cands
    scale = head ** (-0.5) * math.log2(math.e)
    fetch = pltpu.make_async_copy(weight_ref, weight, weight_sem)
    fetch.start()
    greet(place, True)

    sent = []

    def copy(kind, d, half, src, dst, target):
        return pltpu.make_async_remote_copy(
            src_ref=src,
            dst_ref=dst.at[d, half],
            send_sem=red_send.at[kind, d, half],
            recv_sem=red_recv.at[kind, d, half],
            device_id={"ctx": target},
            device_id_type=MESH,
        )

    def go(*what):
        one = copy(*what)
        one.start()
        sent.append(one)

    def arrive(kind, d, half, dst):
        copy(kind, d, half, dst.at[d, half], dst, place.me).wait_recv()

    def owner(d, flip_y, flip_x):
        y = 1 - place.y if flip_y else place.y
        x = 1 - place.x if flip_x else place.x
        return place.at(place.shifted(d), y, x)

    def loader(ref, *index):
        return lambda start, size: ref[(*index, pl.ds(start, size), slice(None))]

    def put(dst, d, half, sums, stats):
        for c in range(combos):
            dst[d, half, c * per : (c + 1) * per, :] = sums[c].astype(BF16)
        dst[d, half, combos * per : (combos + 1) * per, :] = stats.astype(BF16)

    def begin(d):
        go(0, d, 0, parts_ref.at[owner(d, 1, 1), 0], from_diag, place.beside_x)
        go(0, d, 1, parts_ref.at[owner(d, 1, 1), 1], from_diag, place.beside_y)
        go(1, d, 0, parts_ref.at[owner(d, 0, 1), 0], from_x, place.beside_x)
        go(2, d, 1, parts_ref.at[owner(d, 1, 0), 1], from_y, place.beside_y)

    def pass_on(d):
        for half in range(2):
            arrive(0, d, half, from_diag)
            mine = owner(d, 1, 0) if half == 0 else owner(d, 0, 1)
            pieces = (loader(parts_ref, mine, half), loader(from_diag, d, half))
            sums, stats, _ = merge(pieces, combos, per, scale)
            put(to_diag, d, half, sums, stats)
            if half == 0:
                go(2, d, half, to_diag.at[d, half], from_y, place.beside_y)
            else:
                go(1, d, half, to_diag.at[d, half], from_x, place.beside_x)

    def plane(d):
        for half in range(2):
            arrive(1, d, half, from_x)
            arrive(2, d, half, from_y)
            pieces = (
                loader(parts_ref, owner(d, 0, 0), half),
                loader(from_x, d, half),
                loader(from_y, d, half),
            )
            sums, stats, _ = merge(pieces, combos, per, scale)
            put(to_line, d, half, sums, stats)
            if d:
                go(3, d, half, to_line.at[d, half], from_line, place.line(d))

    order = near_first(depth)[::-1] + [0]
    begin(order[0])
    begin(order[1])
    for i, d in enumerate(order):
        pass_on(d)
        if i + 2 < depth:
            begin(order[i + 2])
        if i >= 1:
            plane(order[i - 1])
    plane(order[-1])
    tokens = cands * toks

    def prepare(half):
        for d in range(1, depth):
            arrive(3, d, half, from_line)
        sums, _, denominator = merge(
            [loader(to_line, 0, half)] + [loader(from_line, d, half) for d in range(1, depth)],
            combos,
            per,
            scale,
        )
        denominator = pltpu.roll(denominator, 64, 1)
        for c in range(combos):
            row = (half * combos + c) * per
            ordered[row : row + per, :] = sums[c] / denominator[:, c : c + 1]
        for n in range(kv // 2):
            h, at = half * (kv // 2) + n, n * tokens * group
            block = [
                ordered[pl.ds(h * tokens * group + g, tokens, stride=group), :]
                for g in range(group)
            ]
            gathered[place.me, half, at : at + tokens * group, :] = jnp.concatenate(
                block, axis=0
            ).astype(BF16)

    gather_pieces(place, gathered, send, recv, prepare)
    fetch.wait()
    total[...] = jnp.zeros_like(total)

    def project(i, carry):
        steps = kv * group // 4
        start = pl.multiple_of((i % steps) * 2 * tokens, 2 * tokens)
        both = gathered[:, i // steps, pl.ds(start, 2 * tokens), :].astype(F32)
        left = both[:, :tokens, :].reshape(ranges * tokens, head).astype(BF16)
        right = both[:, tokens:, :].reshape(ranges * tokens, head).astype(BF16)
        rows = pl.multiple_of(i * 2 * head, 2 * head)
        total[...] += jnp.dot(
            jnp.concatenate([left, right], axis=1),
            weight[pl.ds(rows, 2 * head), :],
            preferred_element_type=F32,
        )
        return carry

    lax.fori_loop(0, kv * group // 2, project, 0)
    half = ranges * tokens // 2
    tp = lax.axis_index("tp")
    away[...] = total[pl.ds(pl.multiple_of((1 - tp) * half, half), half), :].astype(BF16)
    swap = pltpu.make_async_remote_copy(
        src_ref=away,
        dst_ref=arrived,
        send_sem=tp_sems.at[0],
        recv_sem=tp_sems.at[1],
        device_id={"tp": 1 - tp},
        device_id_type=MESH,
    )
    swap.start()
    for one in sent:
        one.wait_send()
    swap.wait()
    mine = total[pl.ds(pl.multiple_of(tp * half, half), half), :]
    columns = total.shape[1]
    joined = mine + arrived[...].astype(F32)
    owners, size = ranges // 2, ranges // 2 * toks
    for c in range(columns // 128):
        lines[c, 0] = joined[:, c * 128 : (c + 1) * 128]
        for j in range(cands):
            for t in range(toks):
                lines[c, 1, pl.ds(j * size + t, owners, stride=toks), :] = lines[
                    c, 0, pl.ds(j * toks + t, owners, stride=tokens), :
                ]
            out_ref[j, :, c * 128 : (c + 1) * 128] = lines[
                c, 1, j * size : (j + 1) * size, :
            ].astype(BF16)


def on_device(
    queries,
    cand_keys,
    candidate_values,
    cached_prompt_keys,
    cached_prompt_values,
    block_lists,
    out_weight,
):
    cands, toks, heads, head = queries.shape
    kv = cand_keys.shape[2]
    group = heads // kv
    blocks, block_tokens = cached_prompt_keys.shape[:2]
    ranges = lax.axis_size("ctx")
    depth = ranges // 4
    piece = cands * toks * heads
    per = toks * group
    vmem = pl.BlockSpec(memory_space=pltpu.VMEM)
    limit = 60 * 1024 * 1024

    anywhere = pl.BlockSpec(memory_space=pl.ANY)
    semaphores = [pltpu.SemaphoreType.DMA((4, depth, 2))] * 2
    cache = (blocks, block_tokens * kv, head)
    sorted_cache = (kv, blocks, block_tokens, head)
    everyone, keys, values = pl.pallas_call(
        functools.partial(query_kernel, ranges, kv),
        out_shape=(
            jax.ShapeDtypeStruct((ranges, 2, piece // 2, head), BF16),
            jax.ShapeDtypeStruct(sorted_cache, BF16),
            jax.ShapeDtypeStruct(sorted_cache, BF16),
        ),
        in_specs=[vmem, anywhere, anywhere],
        out_specs=(vmem, anywhere, anywhere),
        scratch_shapes=[
            pltpu.VMEM((2, *cache), BF16),
            pltpu.VMEM((block_tokens * kv, head), F32),
            pltpu.VMEM((2, *sorted_cache), BF16),
            *semaphores,
            pltpu.SemaphoreType.DMA((2,)),
            pltpu.SemaphoreType.DMA((2, 4)),
        ],
        compiler_params=pltpu.CompilerParams(
            collective_id=0, has_side_effects=True, vmem_limit_bytes=limit
        ),
        name="query_gather",
    )(
        queries.reshape(2, piece // 2, head),
        cached_prompt_keys.reshape(cache),
        cached_prompt_values.reshape(cache),
    )

    tile_owners = min(ranges, 256 // per)
    rows = tile_owners * per
    half_rows = piece // 2 + per
    whole = lambda shape: pl.BlockSpec(
        shape, lambda i, *_: (0,) * len(shape), pipeline_mode=pl.Buffered(1)
    )
    own_spec = whole(cand_keys.shape)
    sizes = (cands, toks, kv, group, blocks, block_tokens, head, tile_owners)
    parts = pl.pallas_call(
        functools.partial(attend_kernel, sizes),
        out_shape=jax.ShapeDtypeStruct((ranges, 2, half_rows, head), BF16),
        grid_spec=pltpu.PrefetchScalarGridSpec(
            num_scalar_prefetch=1,
            grid=(ranges // tile_owners,),
            in_specs=[
                whole(block_lists.shape),
                pl.BlockSpec(
                    (tile_owners, cands, toks, heads, head), lambda i, *_: (i, 0, 0, 0, 0)
                ),
                own_spec,
                own_spec,
                anywhere,
                anywhere,
            ],
            out_specs=pl.BlockSpec((tile_owners, 2, half_rows, head), lambda i, *_: (i, 0, 0, 0)),
            scratch_shapes=[
                pltpu.VMEM((kv, blocks, block_tokens, head), BF16),
                pltpu.VMEM((kv, blocks, block_tokens, head), BF16),
                pltpu.VMEM((kv, (blocks + 1) // 2 * 2, rows, block_tokens), F32),
                pltpu.VMEM((kv, rows, block_tokens), F32),
                pltpu.VMEM((kv, rows, head), F32),
                pltpu.VMEM((kv, rows, block_tokens), F32),
                pltpu.SemaphoreType.DMA((2,)),
            ],
        ),
        compiler_params=pltpu.CompilerParams(vmem_limit_bytes=limit),
        name="attend",
    )(
        block_lists,
        block_lists,
        everyone.reshape(ranges, cands, toks, heads, head),
        cand_keys,
        candidate_values,
        keys,
        values,
    )

    columns = out_weight.shape[1]
    tokens = cands * toks
    half = ranges * tokens // 2
    block = pltpu.VMEM((depth, 2, half_rows, head), BF16)
    return pl.pallas_call(
        functools.partial(finish_kernel, ranges, (cands, toks, kv, group, head)),
        out_shape=jax.ShapeDtypeStruct((cands, ranges * toks // 2, columns), BF16),
        in_specs=[vmem, pl.BlockSpec(memory_space=pl.ANY)],
        out_specs=vmem,
        scratch_shapes=[block] * 6
        + [
            pltpu.VMEM((ranges, 2, piece // 2, head), BF16),
            pltpu.VMEM((piece, head), F32),
            pltpu.VMEM(out_weight.shape, BF16),
            pltpu.VMEM((2 * half, columns), F32),
            pltpu.VMEM((half, columns), BF16),
            pltpu.VMEM((half, columns), BF16),
            pltpu.VMEM((columns // 128, 2, half, 128), F32),
            pltpu.SemaphoreType.DMA,
            *semaphores,
            *semaphores,
            pltpu.SemaphoreType.DMA((2,)),
        ],
        compiler_params=pltpu.CompilerParams(
            collective_id=1, has_side_effects=True, vmem_limit_bytes=limit
        ),
        name="reduce_project",
    )(parts, out_weight)


def solution(mesh):
    placed = (
        P("groups", "ctx", "tp", None),
        P("groups", "ctx", "tp", None),
        P("groups", "ctx", "tp", None),
        P(("groups", "ctx"), None, "tp", None),
        P(("groups", "ctx"), None, "tp", None),
        P("groups", None),
        P("tp", "ctx"),
    )
    return jax.shard_map(
        on_device, mesh=mesh, in_specs=placed, out_specs=P("groups", "tp", "ctx"), check_vma=False
    )
```

```python
import functools
import math

import jax
import jax.numpy as jnp
from jax import lax
from jax.experimental import pallas as pl
from jax.experimental.pallas import tpu as pltpu
from jax.sharding import PartitionSpec as P

NEGATIVE = -1e30
MESH = pl.DeviceIdType.MESH
F32, BF16 = jnp.float32, jnp.bfloat16


class Place:
    def __init__(self, ranges):
        self.me = lax.axis_index("ctx")
        self.depth = ranges // 4
        self.x, self.y, self.z = self.me % 2, (self.me // 2) % 2, self.me // 4
        self.beside_x = self.at(self.z, self.y, 1 - self.x)
        self.beside_y = self.at(self.z, 1 - self.y, self.x)

    def at(self, z, y, x):
        return z * 4 + y * 2 + x

    def shifted(self, d):
        return (self.z + d + self.depth) % self.depth

    def line(self, d):
        return self.at(self.shifted(d), self.y, self.x)


def greet(place, with_tp):
    barrier = pltpu.get_barrier_semaphore()
    others = [place.line(d) for d in range(1, place.depth)]
    for other in others + [place.beside_x, place.beside_y]:
        pl.semaphore_signal(barrier, inc=1, device_id={"ctx": other}, device_id_type=MESH)
    if with_tp:
        pl.semaphore_signal(
            barrier, inc=1, device_id={"tp": 1 - lax.axis_index("tp")}, device_id_type=MESH
        )
    pl.semaphore_wait(barrier, place.depth + 1 + int(with_tp))


def near_first(depth):
    order = []
    for step in range(1, depth // 2 + 1):
        order += [step] + ([depth - step] if depth - step != step else [])
    return order


def gather_pieces(place, buf, send, recv, prepare, work=lambda step: None):
    def copy(kind, d, half, owner, target):
        return pltpu.make_async_remote_copy(
            src_ref=buf.at[owner, half],
            dst_ref=buf.at[owner, half],
            send_sem=send.at[kind, d, half],
            recv_sem=recv.at[kind, d, half],
            device_id={"ctx": target},
            device_id_type=MESH,
        )

    sent = []

    def go(*what):
        one = copy(*what)
        one.start()
        sent.append(one)

    depth = place.depth
    z_of = [place.shifted(-d) for d in range(depth)]

    def spread(d, half):
        owner = place.at(z_of[d], place.y, place.x)
        if d:
            copy(0, d, half, owner, place.me).wait_recv()
        go(1, d, half, owner, place.beside_x)
        go(2, d, half, owner, place.beside_y)

    def relay(d, half):
        from_x = place.at(z_of[d], place.y, 1 - place.x)
        from_y = place.at(z_of[d], 1 - place.y, place.x)
        if half == 0:
            copy(1, d, half, from_x, place.me).wait_recv()
            go(3, d, half, from_x, place.beside_y)
        else:
            copy(2, d, half, from_y, place.me).wait_recv()
            go(3, d, half, from_y, place.beside_x)

    def settle(d, half):
        from_x = place.at(z_of[d], place.y, 1 - place.x)
        from_y = place.at(z_of[d], 1 - place.y, place.x)
        if half == 0:
            copy(2, d, half, from_y, place.me).wait_recv()
        else:
            copy(1, d, half, from_x, place.me).wait_recv()
        across = place.at(z_of[d], 1 - place.y, 1 - place.x)
        copy(3, d, half, across, place.me).wait_recv()

    order = near_first(depth)
    for half in range(2):
        prepare(half)
        spread(0, half)
        for d in order:
            go(0, d, half, place.me, place.line(d))
    work(0)
    steps = [(d, half) for d in [0] + order for half in range(2)]
    for i, step in enumerate(steps):
        if i + 2 < len(steps):
            spread(*steps[i + 2])
        relay(*step)
        work(i + 1)
    for step in steps:
        settle(*step)
    for one in sent:
        one.wait_send()


def query_kernel(
    ranges,
    kv,
    q_ref,
    k_ref,
    v_ref,
    out_ref,
    k_out,
    v_out,
    raw,
    wide,
    heads,
    send,
    recv,
    in_sems,
    out_sems,
):
    place = Place(ranges)
    sources, results = (k_ref, v_ref), (k_out, v_out)
    fetches = [pltpu.make_async_copy(sources[n], raw.at[n], in_sems.at[n]) for n in range(2)]
    for fetch in fetches:
        fetch.start()
    out_ref[place.me] = q_ref[...]
    greet(place, False)
    prepare = lambda half: None
    blocks, block_tokens = raw.shape[1], raw.shape[2] // kv
    parts = 4
    per = blocks // parts
    stores = []

    def work(step):
        if step >= 2 * parts:
            return
        n, part = step // parts, step % parts
        if part == 0:
            fetches[n].wait()

        def one(b, carry):
            wide[...] = raw[n, b].astype(F32)
            for h in range(kv):
                heads[n, h, b] = wide[pl.ds(h, block_tokens, stride=kv), :].astype(BF16)
            return carry

        lax.fori_loop(part * per, (part + 1) * per, one, 0)
        some = pl.ds(part * per, per)
        store = pltpu.make_async_copy(
            heads.at[n, :, some], results[n].at[:, some], out_sems.at[n, part]
        )
        store.start()
        stores.append(store)

    gather_pieces(place, out_ref, send, recv, prepare, work)
    for store in stores:
        store.wait()


def attend_kernel(
    sizes,
    lists_smem,
    lists_ref,
    q_ref,
    own_k_ref,
    own_v_ref,
    k_ref,
    v_ref,
    out_ref,
    k_heads,
    v_heads,
    scores,
    sums,
    acc,
    top,
    sems,
):
    cands, toks, kv, group, blocks, block_tokens, head, tile_owners = sizes
    chunk = pl.program_id(0)
    me = lax.axis_index("ctx")
    scale = head ** (-0.5) * math.log2(math.e)
    rows = tile_owners * toks * group
    lowest = me * blocks

    fetch_k = pltpu.make_async_copy(k_ref, k_heads, sems.at[0])
    fetch_v = pltpu.make_async_copy(v_ref, v_heads, sems.at[1])

    @pl.when(chunk == 0)
    def _():
        fetch_k.start()
        fetch_v.start()

    key_row = lax.broadcasted_iota(jnp.int32, (block_tokens, head), 0)

    def own_block(ref, h, j):
        rows_here = ref[j].astype(F32)
        block = jnp.zeros((block_tokens, head), F32)
        for t in range(toks):
            block = jnp.where(key_row == t, rows_here[t, h : h + 1, :], block)
        return block.astype(BF16)

    row = lax.broadcasted_iota(jnp.int32, (rows, block_tokens), 0)
    lane = lax.broadcasted_iota(jnp.int32, (rows, block_tokens), 1)
    query_pos = chunk * tile_owners * toks + row // group
    own_seen = (lane < toks) & (me * toks + lane <= query_pos)
    stats = [jnp.zeros((rows, 128), F32)] * 2
    per = toks * group
    lanes = lax.broadcasted_iota(jnp.int32, (rows, 128), 1)
    nt = (((1,), (1,)), ((), ()))
    for j in range(cands):
        line = lists_ref[j : j + 1, :]
        below = jnp.sum((line < lowest).astype(jnp.int32))
        count = jnp.sum((line < lowest + blocks).astype(jnp.int32)) - below
        last = lists_smem.shape[1] - 1

        def listed(slot):
            return lists_smem[j, jnp.minimum(below + slot, last)] - lowest

        fours = count // 4
        pairs = (count - 4 * fours + 1) // 2

        def four_of(i):
            return 4 * i, [listed(4 * i + n) for n in range(4)], None

        def pair_of(i):
            slot = 4 * fours + 2 * i
            inside = slot + 1 < count
            first = listed(slot)
            return slot, [first, jnp.where(inside, listed(slot + 1), first)], inside

        def scores_of(h, picked):
            keys = jnp.concatenate([k_heads[h, b] for b in picked], axis=0)
            s = lax.dot_general(queries[h], keys, nt, preferred_element_type=F32)
            return [s[:, n * block_tokens : (n + 1) * block_tokens] for n in range(len(picked))]

        queries = []
        for h in range(kv):
            q = q_ref[:, j, :, h * group : (h + 1) * group, :].astype(F32)
            queries.append(q.reshape(rows, head).astype(BF16))
            own = lax.dot_general(
                queries[h], own_block(own_k_ref, h, j), nt, preferred_element_type=F32
            )
            own = jnp.where(own_seen, own, NEGATIVE)
            sums[h] = own
            top[h] = own

        if j == 0:
            pl.when(chunk == 0)(fetch_k.wait)

        def first_pass(pick, i, carry):
            slot, picked, _ = pick(i)
            for h in range(kv):
                found = scores_of(h, picked)
                for n, s in enumerate(found):
                    scores[h, slot + n] = s
                top[h] = functools.reduce(jnp.maximum, found, top[h])
            return carry

        lax.fori_loop(0, fours, functools.partial(first_pass, four_of), 0)
        lax.fori_loop(0, pairs, functools.partial(first_pass, pair_of), 0)
        for h in range(kv):
            peak = jnp.max(top[h], axis=1, keepdims=True).astype(BF16).astype(F32)
            p = jnp.where(own_seen, jnp.exp2((sums[h] - peak) * scale), 0.0)
            sums[h] = p
            acc[h] = jnp.dot(
                p.astype(BF16), own_block(own_v_ref, h, j), preferred_element_type=F32
            )
            top[h] = jnp.broadcast_to(peak, (rows, block_tokens))

        def second_pass(pick, i, carry):
            slot, picked, inside = pick(i)
            for h in range(kv):
                peak = top[h]
                p = [
                    jnp.exp2((scores[h, slot + n] - peak) * scale) for n in range(len(picked))
                ]
                if inside is not None:
                    p[-1] = jnp.where(inside, p[-1], 0.0)
                sums[h] += functools.reduce(jnp.add, p)
                values = jnp.concatenate([v_heads[h, b] for b in picked], axis=0)
                weights = jnp.concatenate([one.astype(BF16) for one in p], axis=1)
                acc[h] += jnp.dot(weights, values, preferred_element_type=F32)
            return carry

        if j == 0:
            pl.when(chunk == 0)(fetch_v.wait)
        lax.fori_loop(0, fours, functools.partial(second_pass, four_of), 0)
        lax.fori_loop(0, pairs, functools.partial(second_pass, pair_of), 0)
        for h in range(kv):
            half, combo = h // (kv // 2), (h % (kv // 2)) * cands + j
            total = jnp.sum(sums[h], axis=1, keepdims=True)
            stats[half] = jnp.where(lanes == combo, top[h], stats[half])
            stats[half] = jnp.where(lanes == 64 + combo, total, stats[half])
            out_ref[:, half, combo * per : (combo + 1) * per, :] = (
                acc[h].reshape(tile_owners, per, head).astype(BF16)
            )
    full = kv // 2 * cands * per
    for half in range(2):
        out_ref[:, half, full : full + per, :] = (
            stats[half].reshape(tile_owners, per, 128).astype(BF16)
        )


def merge(pieces, combos, per, scale):
    full = combos * per
    stats = [load(full, per).astype(F32) for load in pieces]
    peak = functools.reduce(jnp.maximum, stats)
    low = lax.broadcasted_iota(jnp.int32, (per, 128), 1) < 64
    scales = [jnp.exp2((jnp.where(low, s - peak, 0.0)) * scale) for s in stats]
    total = sum(pltpu.roll(w, 64, 1) * s for w, s in zip(scales, stats))
    sums = []
    for c in range(combos):
        sums.append(
            sum(
                load(c * per, per).astype(F32) * w[:, c : c + 1]
                for load, w in zip(pieces, scales)
            )
        )
    return sums, jnp.where(low, peak, total), total


def finish_kernel(
    ranges,
    sizes,
    parts_ref,
    weight_ref,
    out_ref,
    from_diag,
    from_x,
    from_y,
    from_line,
    to_diag,
    to_line,
    gathered,
    ordered,
    weight,
    total,
    away,
    arrived,
    lines,
    weight_sem,
    red_send,
    red_recv,
    send,
    recv,
    tp_sems,
):
    cands, toks, kv, group, head = sizes
    place = Place(ranges)
    depth = place.depth
    per = toks * group
    combos = kv // 2 * cands
    scale = head ** (-0.5) * math.log2(math.e)
    fetch = pltpu.make_async_copy(weight_ref, weight, weight_sem)
    fetch.start()
    greet(place, True)

    sent = []

    def copy(kind, d, half, src, dst, target):
        return pltpu.make_async_remote_copy(
            src_ref=src,
            dst_ref=dst.at[d, half],
            send_sem=red_send.at[kind, d, half],
            recv_sem=red_recv.at[kind, d, half],
            device_id={"ctx": target},
            device_id_type=MESH,
        )

    def go(*what):
        one = copy(*what)
        one.start()
        sent.append(one)

    def arrive(kind, d, half, dst):
        copy(kind, d, half, dst.at[d, half], dst, place.me).wait_recv()

    def owner(d, flip_y, flip_x):
        y = 1 - place.y if flip_y else place.y
        x = 1 - place.x if flip_x else place.x
        return place.at(place.shifted(d), y, x)

    def loader(ref, *index):
        return lambda start, size: ref[(*index, pl.ds(start, size), slice(None))]

    def put(dst, d, half, sums, stats):
        for c in range(combos):
            dst[d, half, c * per : (c + 1) * per, :] = sums[c].astype(BF16)
        dst[d, half, combos * per : (combos + 1) * per, :] = stats.astype(BF16)

    def begin(d):
        go(0, d, 0, parts_ref.at[owner(d, 1, 1), 0], from_diag, place.beside_x)
        go(0, d, 1, parts_ref.at[owner(d, 1, 1), 1], from_diag, place.beside_y)
        go(1, d, 0, parts_ref.at[owner(d, 0, 1), 0], from_x, place.beside_x)
        go(2, d, 1, parts_ref.at[owner(d, 1, 0), 1], from_y, place.beside_y)

    def pass_on(d):
        for half in range(2):
            arrive(0, d, half, from_diag)
            mine = owner(d, 1, 0) if half == 0 else owner(d, 0, 1)
            pieces = (loader(parts_ref, mine, half), loader(from_diag, d, half))
            sums, stats, _ = merge(pieces, combos, per, scale)
            put(to_diag, d, half, sums, stats)
            if half == 0:
                go(2, d, half, to_diag.at[d, half], from_y, place.beside_y)
            else:
                go(1, d, half, to_diag.at[d, half], from_x, place.beside_x)

    def plane(d):
        for half in range(2):
            arrive(1, d, half, from_x)
            arrive(2, d, half, from_y)
            pieces = (
                loader(parts_ref, owner(d, 0, 0), half),
                loader(from_x, d, half),
                loader(from_y, d, half),
            )
            sums, stats, _ = merge(pieces, combos, per, scale)
            put(to_line, d, half, sums, stats)
            if d:
                go(3, d, half, to_line.at[d, half], from_line, place.line(d))

    order = near_first(depth)[::-1] + [0]
    begin(order[0])
    begin(order[1])
    for i, d in enumerate(order):
        pass_on(d)
        if i + 2 < depth:
            begin(order[i + 2])
        if i >= 1:
            plane(order[i - 1])
    plane(order[-1])
    tokens = cands * toks

    def prepare(half):
        for d in range(1, depth):
            arrive(3, d, half, from_line)
        sums, _, denominator = merge(
            [loader(to_line, 0, half)] + [loader(from_line, d, half) for d in range(1, depth)],
            combos,
            per,
            scale,
        )
        denominator = pltpu.roll(denominator, 64, 1)
        for c in range(combos):
            row = (half * combos + c) * per
            ordered[row : row + per, :] = sums[c] / denominator[:, c : c + 1]
        for n in range(kv // 2):
            h, at = half * (kv // 2) + n, n * tokens * group
            block = [
                ordered[pl.ds(h * tokens * group + g, tokens, stride=group), :]
                for g in range(group)
            ]
            gathered[place.me, half, at : at + tokens * group, :] = jnp.concatenate(
                block, axis=0
            ).astype(BF16)

    gather_pieces(place, gathered, send, recv, prepare)
    fetch.wait()
    total[...] = jnp.zeros_like(total)

    def project(i, carry):
        steps = kv * group // 4
        start = pl.multiple_of((i % steps) * 2 * tokens, 2 * tokens)
        both = gathered[:, i // steps, pl.ds(start, 2 * tokens), :].astype(F32)
        left = both[:, :tokens, :].reshape(ranges * tokens, head).astype(BF16)
        right = both[:, tokens:, :].reshape(ranges * tokens, head).astype(BF16)
        rows = pl.multiple_of(i * 2 * head, 2 * head)
        total[...] += jnp.dot(
            jnp.concatenate([left, right], axis=1),
            weight[pl.ds(rows, 2 * head), :],
            preferred_element_type=F32,
        )
        return carry

    lax.fori_loop(0, kv * group // 2, project, 0)
    half = ranges * tokens // 2
    tp = lax.axis_index("tp")
    away[...] = total[pl.ds(pl.multiple_of((1 - tp) * half, half), half), :].astype(BF16)
    swap = pltpu.make_async_remote_copy(
        src_ref=away,
        dst_ref=arrived,
        send_sem=tp_sems.at[0],
        recv_sem=tp_sems.at[1],
        device_id={"tp": 1 - tp},
        device_id_type=MESH,
    )
    swap.start()
    for one in sent:
        one.wait_send()
    swap.wait()
    mine = total[pl.ds(pl.multiple_of(tp * half, half), half), :]
    columns = total.shape[1]
    joined = mine + arrived[...].astype(F32)
    owners, size = ranges // 2, ranges // 2 * toks
    for c in range(columns // 128):
        lines[c, 0] = joined[:, c * 128 : (c + 1) * 128]
        for j in range(cands):
            for t in range(toks):
                lines[c, 1, pl.ds(j * size + t, owners, stride=toks), :] = lines[
                    c, 0, pl.ds(j * toks + t, owners, stride=tokens), :
                ]
            out_ref[j, :, c * 128 : (c + 1) * 128] = lines[
                c, 1, j * size : (j + 1) * size, :
            ].astype(BF16)


def on_device(
    queries,
    cand_keys,
    candidate_values,
    cached_prompt_keys,
    cached_prompt_values,
    block_lists,
    out_weight,
):
    cands, toks, heads, head = queries.shape
    kv = cand_keys.shape[2]
    group = heads // kv
    blocks, block_tokens = cached_prompt_keys.shape[:2]
    ranges = lax.axis_size("ctx")
    depth = ranges // 4
    piece = cands * toks * heads
    per = toks * group
    vmem = pl.BlockSpec(memory_space=pltpu.VMEM)
    limit = 60 * 1024 * 1024

    anywhere = pl.BlockSpec(memory_space=pl.ANY)
    semaphores = [pltpu.SemaphoreType.DMA((4, depth, 2))] * 2
    cache = (blocks, block_tokens * kv, head)
    sorted_cache = (kv, blocks, block_tokens, head)
    everyone, keys, values = pl.pallas_call(
        functools.partial(query_kernel, ranges, kv),
        out_shape=(
            jax.ShapeDtypeStruct((ranges, 2, piece // 2, head), BF16),
            jax.ShapeDtypeStruct(sorted_cache, BF16),
            jax.ShapeDtypeStruct(sorted_cache, BF16),
        ),
        in_specs=[vmem, anywhere, anywhere],
        out_specs=(vmem, anywhere, anywhere),
        scratch_shapes=[
            pltpu.VMEM((2, *cache), BF16),
            pltpu.VMEM((block_tokens * kv, head), F32),
            pltpu.VMEM((2, *sorted_cache), BF16),
            *semaphores,
            pltpu.SemaphoreType.DMA((2,)),
            pltpu.SemaphoreType.DMA((2, 4)),
        ],
        compiler_params=pltpu.CompilerParams(
            collective_id=0, has_side_effects=True, vmem_limit_bytes=limit
        ),
        name="query_gather",
    )(
        queries.reshape(2, piece // 2, head),
        cached_prompt_keys.reshape(cache),
        cached_prompt_values.reshape(cache),
    )

    tile_owners = min(ranges, 256 // per)
    rows = tile_owners * per
    half_rows = piece // 2 + per
    whole = lambda shape: pl.BlockSpec(
        shape, lambda i, *_: (0,) * len(shape), pipeline_mode=pl.Buffered(1)
    )
    own_spec = whole(cand_keys.shape)
    sizes = (cands, toks, kv, group, blocks, block_tokens, head, tile_owners)
    parts = pl.pallas_call(
        functools.partial(attend_kernel, sizes),
        out_shape=jax.ShapeDtypeStruct((ranges, 2, half_rows, head), BF16),
        grid_spec=pltpu.PrefetchScalarGridSpec(
            num_scalar_prefetch=1,
            grid=(ranges // tile_owners,),
            in_specs=[
                whole(block_lists.shape),
                pl.BlockSpec(
                    (tile_owners, cands, toks, heads, head), lambda i, *_: (i, 0, 0, 0, 0)
                ),
                own_spec,
                own_spec,
                anywhere,
                anywhere,
            ],
            out_specs=pl.BlockSpec((tile_owners, 2, half_rows, head), lambda i, *_: (i, 0, 0, 0)),
            scratch_shapes=[
                pltpu.VMEM((kv, blocks, block_tokens, head), BF16),
                pltpu.VMEM((kv, blocks, block_tokens, head), BF16),
                pltpu.VMEM((kv, (blocks + 1) // 2 * 2, rows, block_tokens), F32),
                pltpu.VMEM((kv, rows, block_tokens), F32),
                pltpu.VMEM((kv, rows, head), F32),
                pltpu.VMEM((kv, rows, block_tokens), F32),
                pltpu.SemaphoreType.DMA((2,)),
            ],
        ),
        compiler_params=pltpu.CompilerParams(vmem_limit_bytes=limit),
        name="attend",
    )(
        block_lists,
        block_lists,
        everyone.reshape(ranges, cands, toks, heads, head),
        cand_keys,
        candidate_values,
        keys,
        values,
    )

    columns = out_weight.shape[1]
    tokens = cands * toks
    half = ranges * tokens // 2
    block = pltpu.VMEM((depth, 2, half_rows, head), BF16)
    return pl.pallas_call(
        functools.partial(finish_kernel, ranges, (cands, toks, kv, group, head)),
        out_shape=jax.ShapeDtypeStruct((cands, ranges * toks // 2, columns), BF16),
        in_specs=[vmem, pl.BlockSpec(memory_space=pl.ANY)],
        out_specs=vmem,
        scratch_shapes=[block] * 6
        + [
            pltpu.VMEM((ranges, 2, piece // 2, head), BF16),
            pltpu.VMEM((piece, head), F32),
            pltpu.VMEM(out_weight.shape, BF16),
            pltpu.VMEM((2 * half, columns), F32),
            pltpu.VMEM((half, columns), BF16),
            pltpu.VMEM((half, columns), BF16),
            pltpu.VMEM((columns // 128, 2, half, 128), F32),
            pltpu.SemaphoreType.DMA,
            *semaphores,
            *semaphores,
            pltpu.SemaphoreType.DMA((2,)),
        ],
        compiler_params=pltpu.CompilerParams(
            collective_id=1, has_side_effects=True, vmem_limit_bytes=limit
        ),
        name="reduce_project",
    )(parts, out_weight)


def solution(mesh):
    placed = (
        P("groups", "ctx", "tp", None),
        P("groups", "ctx", "tp", None),
        P("groups", "ctx", "tp", None),
        P(("groups", "ctx"), None, "tp", None),
        P(("groups", "ctx"), None, "tp", None),
        P("groups", None),
        P("tp", "ctx"),
    )
    return jax.shard_map(
        on_device, mesh=mesh, in_specs=placed, out_specs=P("groups", "tp", "ctx"), check_vma=False
    )
```
